32 devices in a mesh: dp: 16 (over z, x, core), ctx: 2 (over y).
Axes of the slice: x: 2, y: 2, z: 4, core: 2. Of those that a mesh axis runs over, the one named last changes fastest.
Arguments:
- tokens: bfloat16 [32768, 1024], P(('dp', 'ctx')), may hold values from -6 to 6
- cotangent: bfloat16 [32768, 1024], P(('dp', 'ctx')), may hold values from -6 to 6
- pair_order: int32 [16, 2], P('dp'), may hold values from 0 to 1, each once within a row
- qkv_weight: float32 [1024, 3072], P(('dp', 'ctx')), may hold values from -0.1875 to 0.1875
- qkv_momentum: float32 [1024, 3072], P(('dp', 'ctx')), may hold values from -0.03125 to 0.03125
- qkv_average: float32 [1024, 3072], P(('dp', 'ctx')), may hold values from -0.1875 to 0.1875
- out_weight: float32 [1024, 1024], P(('dp', 'ctx')), may hold values from -0.1875 to 0.1875
- out_momentum: float32 [1024, 1024], P(('dp', 'ctx')), may hold values from -0.03125 to 0.03125
- out_average: float32 [1024, 1024], P(('dp', 'ctx')), may hold values from -0.1875 to 0.1875
- up_weight: float32 [1024, 4096], P(('dp', 'ctx')), may hold values from -0.1875 to 0.1875
- up_momentum: float32 [1024, 4096], P(('dp', 'ctx')), may hold values from -0.03125 to 0.03125
- up_average: float32 [1024, 4096], P(('dp', 'ctx')), may hold values from -0.1875 to 0.1875
- down_weight: float32 [4096, 1024], P(('dp', 'ctx')), may hold values from -0.09375 to 0.09375
- down_momentum: float32 [4096, 1024], P(('dp', 'ctx')), may hold values from -0.03125 to 0.03125
- down_average: float32 [4096, 1024], P(('dp', 'ctx')), may hold values from -0.09375 to 0.09375
- norm_weight: float32 [8, 1024], P(None, ('dp', 'ctx')), may hold values from -1.2 to 1.45
- norm_momentum: float32 [8, 1024], P(None, ('dp', 'ctx')), may hold values from -0.03125 to 0.03125
- norm_average: float32 [8, 1024], P(None, ('dp', 'ctx')), may hold values from -1.2 to 1.45
Outputs:
- output: bfloat16 [32768, 1024], P(('dp', 'ctx'))
- input_grad: bfloat16 [32768, 1024], P(('dp', 'ctx'))
- qkv_momentum_new: float32 [1024, 3072], P(('dp', 'ctx'))
- qkv_weight_new: float32 [1024, 3072], P(('dp', 'ctx'))
- qkv_average_new: float32 [1024, 3072], P(('dp', 'ctx'))
- out_momentum_new: float32 [1024, 1024], P(('dp', 'ctx'))
- out_weight_new: float32 [1024, 1024], P(('dp', 'ctx'))
- out_average_new: float32 [1024, 1024], P(('dp', 'ctx'))
- up_momentum_new: float32 [1024, 4096], P(('dp', 'ctx'))
- up_weight_new: float32 [1024, 4096], P(('dp', 'ctx'))
- up_average_new: float32 [1024, 4096], P(('dp', 'ctx'))
- down_momentum_new: float32 [4096, 1024], P(('dp', 'ctx'))
- down_weight_new: float32 [4096, 1024], P(('dp', 'ctx'))
- down_average_new: float32 [4096, 1024], P(('dp', 'ctx'))
- norm_momentum_new: float32 [8, 1024], P(None, ('dp', 'ctx'))
- norm_weight_new: float32 [8, 1024], P(None, ('dp', 'ctx'))
- norm_average_new: float32 [8, 1024], P(None, ('dp', 'ctx'))
The draws below stay inside these ranges and needn't reach their ends.
Inputs may be any that keep to these rules, and one draw needn't show every extreme that they name: `pair_order`: each row holds every pair number once.
All inputs are finite; a program needn't handle non-finite values.
Results may differ from the reference program's by a relative error of at most 0.01.
Values may be sent and summed in bfloat16 or wider, within the bound.
No kernel may reach another device: no remote copies, remote signals or barrier semaphores. Data moves between devices by JAX's collectives and lax.ppermute only.
A program may use at most 320 MiB of HBM per device.

```python
import math
import jax
import jax.numpy as jnp
from jax import lax

D = 1024
HEADS = 16
HEAD_DIM = 64
FF = 4096
SEQ = 2048
SEQS = 1
SEQS_ALL = 16
TOKENS = 32768
N_DP = 16
N_CTX = 2


def norm_table(base_key):
    normal_vals = jax.random.normal(base_key, (8, D), jnp.float32)
    row_kind = jnp.arange(8)[:, None] % 2
    gains = 1.0 + 0.15 * jnp.clip(normal_vals, -3.0, 3.0)
    shifts = 0.3 * jnp.clip(normal_vals, -4.0, 4.0)
    return jnp.where(row_kind == 0, gains, shifts)


def draw_norm_weight(key, part):
    return norm_table(jax.random.fold_in(key, 11))


def draw_norm_average(key, part):
    return norm_table(jax.random.fold_in(key, 12))


def levels(rng, extent, pieces, smallest, largest):
    loudness, own = 1.0, jax.random.fold_in(rng, 6)
    for dim, shards_of in pieces:
        heights = jnp.exp(jax.random.uniform(jax.random.fold_in(own, dim), (shards_of,), jnp.float32, smallest / len(pieces), largest / len(pieces)))
        loudness = loudness * jnp.repeat(heights, extent[dim] // shards_of).reshape([-1 if axis == dim else 1 for axis in range(len(extent))])
    return loudness


def scatter_about(rng, shape, width, bound, split=(), kind=jnp.bfloat16):
    factor_of = levels(rng, shape, split, -0.22, 0.18) if split else 1.0
    array = jax.random.normal(rng, shape, jnp.float32) * width * factor_of
    return jnp.minimum(jnp.maximum(array, -bound), bound).astype(kind)


def setup_inputs(seed: int = 0) -> dict:
    streams_of = jax.random.split(jax.random.key(seed), 19)
    return {
        "tokens": scatter_about(streams_of[0], (TOKENS, D), 1.0, 6.0, ((0, 32),)),
        "cotangent": scatter_about(streams_of[1], (TOKENS, D), 1.0, 6.0, ((0, 32),)),
        "pair_order": jax.vmap(lambda own: jax.random.permutation(own, N_CTX))(jax.random.split(streams_of[2], SEQS_ALL)).reshape((SEQS_ALL, N_CTX)).astype(jnp.int32),
        "qkv_weight": scatter_about(streams_of[3], (D, 3 * D), D ** -0.5, 0.1875, ((0, 32),), jnp.float32),
        "qkv_momentum": scatter_about(streams_of[4], (D, 3 * D), TOKENS ** -0.5, 0.03125, ((0, 32),), jnp.float32),
        "qkv_average": scatter_about(streams_of[5], (D, 3 * D), D ** -0.5, 0.1875, ((0, 32),), jnp.float32),
        "out_weight": scatter_about(streams_of[6], (D, D), D ** -0.5, 0.1875, ((0, 32),), jnp.float32),
        "out_momentum": scatter_about(streams_of[7], (D, D), TOKENS ** -0.5, 0.03125, ((0, 32),), jnp.float32),
        "out_average": scatter_about(streams_of[8], (D, D), D ** -0.5, 0.1875, ((0, 32),), jnp.float32),
        "up_weight": scatter_about(streams_of[9], (D, FF), D ** -0.5, 0.1875, ((0, 32),), jnp.float32),
        "up_momentum": scatter_about(streams_of[10], (D, FF), TOKENS ** -0.5, 0.03125, ((0, 32),), jnp.float32),
        "up_average": scatter_about(streams_of[11], (D, FF), D ** -0.5, 0.1875, ((0, 32),), jnp.float32),
        "down_weight": scatter_about(streams_of[12], (FF, D), FF ** -0.5, 0.09375, ((0, 32),), jnp.float32),
        "down_momentum": scatter_about(streams_of[13], (FF, D), TOKENS ** -0.5, 0.03125, ((0, 32),), jnp.float32),
        "down_average": scatter_about(streams_of[14], (FF, D), FF ** -0.5, 0.09375, ((0, 32),), jnp.float32),
        "norm_weight": draw_norm_weight(jax.random.fold_in(streams_of[18], 71), 0),
        "norm_momentum": scatter_about(streams_of[16], (8, D), TOKENS ** -0.5, 0.03125, ((1, 32),), jnp.float32),
        "norm_average": draw_norm_average(jax.random.fold_in(streams_of[18], 71), 0),
    }


@jax.custom_vjp
def low(v):
    return lax.optimization_barrier(v.astype(jnp.bfloat16)).astype(jnp.float32)

@jax.custom_vjp
def low_back(v):
    return v

def low_keep(v):
    return (low(v), None)

def low_pass(kept, grad):
    return (grad,)

def back_keep(v):
    return (v, None)

def back_low(kept, grad):
    return (low(grad),)
low.defvjp(low_keep, low_pass)
low_back.defvjp(back_keep, back_low)
highest = lax.Precision.HIGHEST
rate_qkv = 0.04
rate_out = 0.03
rate_up = 0.03
rate_down = 0.02
rate_norm = 0.3

def layer_norm(values, gain_row, shift_row):
    centre = values - lax.optimization_barrier(jnp.mean(values, axis=-1, keepdims=True))
    spread = lax.optimization_barrier(jnp.mean(centre * centre, axis=-1, keepdims=True))
    return centre * lax.rsqrt(spread + 1e-05) * gain_row + shift_row

def rotary_tables(positions):
    half_dim = HEAD_DIM // 2
    frequency = jnp.exp(jnp.arange(half_dim, dtype=jnp.float32) * (-math.log(10000.0) / half_dim))
    angles = positions.astype(jnp.float32)[:, None] * frequency[None, :]
    angles = jnp.concatenate([angles, angles], axis=1)
    return (jnp.cos(angles), jnp.sin(angles))

def rotary(values, cos_table, sin_table):
    shaped = values.reshape(values.shape[0], HEADS, HEAD_DIM)
    half_dim = HEAD_DIM // 2
    turned = jnp.concatenate([-shaped[:, :, half_dim:], shaped[:, :, :half_dim]], axis=2)
    result = shaped * cos_table[:, None, :] + turned * sin_table[:, None, :]
    return result.reshape(values.shape)

def matmul(left_side, right_side):
    return jnp.dot(left_side, right_side, precision=highest, preferred_element_type=jnp.float32)

def one_sequence(params, sequence, positions):
    w_qkv, w_out, w_up, w_down, norm_rows = params
    score_scale = 1.0 / math.sqrt(HEAD_DIM)
    cos_table, sin_table = rotary_tables(positions)
    attn_in = low(layer_norm(sequence, norm_rows[0], norm_rows[1]))
    qkv_rows = low_back(matmul(attn_in, w_qkv))
    queries = low(rotary(qkv_rows[:, :D], cos_table, sin_table)).reshape(SEQ, HEADS, HEAD_DIM)
    key_heads = low(rotary(qkv_rows[:, D:2 * D], cos_table, sin_table)).reshape(SEQ, HEADS, HEAD_DIM)
    value_heads = low(qkv_rows[:, 2 * D:]).reshape(SEQ, HEADS, HEAD_DIM)
    scores = low_back(jnp.einsum('qhe,khe->hqk', queries, key_heads, precision=highest) * score_scale)
    allowed = positions[None, :] <= positions[:, None]
    scores = jnp.where(allowed[None], scores, -jnp.inf)
    row_top = lax.optimization_barrier(jnp.max(scores, axis=2, keepdims=True))
    weights = jnp.exp(scores - row_top)
    prob_low = low(weights / lax.optimization_barrier(jnp.sum(weights, axis=2, keepdims=True)))
    mixed_rows = jnp.einsum('hqk,khe->qhe', prob_low, value_heads, precision=highest).reshape(SEQ, D)
    mixed_rows = low(low_back(mixed_rows))
    projected = low_back(matmul(mixed_rows, w_out))
    hidden = sequence + layer_norm(projected, norm_rows[2], norm_rows[3])
    mlp_in = low(layer_norm(hidden, norm_rows[4], norm_rows[5]))
    up_rows = low_back(matmul(mlp_in, w_up))
    active = low(jax.nn.gelu(up_rows))
    down_rows = low_back(matmul(active, w_down))
    return hidden + layer_norm(down_rows, norm_rows[6], norm_rows[7])

def forward(token_vals, w_qkv, w_out, w_up, w_down, norm_rows, positions):
    params = (low(w_qkv), low(w_out), low(w_up), low(w_down), low(norm_rows))
    checked = jax.checkpoint(one_sequence)
    return lax.map(lambda item_pair: checked(params, item_pair[0], item_pair[1]), (token_vals, positions))

def nesterov(gradient, momentum, weight, average, step_rate):
    scaled = gradient / TOKENS
    new_momentum = 0.5 * momentum + scaled
    new_weight = weight - step_rate * math.sqrt(TOKENS) * (scaled + 0.5 * new_momentum)
    new_average = 0.5 * average + 0.5 * new_weight
    return (new_momentum, new_weight, new_average)

def reference(tokens, cotangent, pair_order, qkv_weight, qkv_momentum, qkv_average, out_weight, out_momentum, out_average, up_weight, up_momentum, up_average, down_weight, down_momentum, down_average, norm_weight, norm_momentum, norm_average):
    span_len = SEQ // (2 * N_CTX)
    block_len = SEQ // N_CTX
    halves = jnp.arange(2, dtype=jnp.int32)
    span_ids = jnp.where(halves[None, None, :] == 0, pair_order[:, :, None], 2 * N_CTX - 1 - pair_order[:, :, None])
    positions = (span_ids[:, :, :, None] * span_len + jnp.arange(span_len, dtype=jnp.int32)[None, None, None, :]).reshape(SEQS_ALL, SEQ)

    def to_sequences(stacked):
        return stacked.astype(jnp.float32).reshape(N_DP, N_CTX, SEQS, block_len, D).transpose(0, 2, 1, 3, 4).reshape(SEQS_ALL, SEQ, D)

    def to_rows(stacked):
        return stacked.reshape(N_DP, SEQS, N_CTX, block_len, D).transpose(0, 2, 1, 3, 4).reshape(TOKENS, D)

    def whole_layer(token_vals, w_qkv, w_out, w_up, w_down, norm_rows):
        return forward(token_vals, w_qkv, w_out, w_up, w_down, norm_rows, positions)
    result, pullback = jax.vjp(whole_layer, to_sequences(tokens), qkv_weight, out_weight, up_weight, down_weight, norm_weight)
    gradients = pullback(to_sequences(cotangent))
    output = to_rows(result).astype(jnp.bfloat16)
    input_grad = to_rows(gradients[0]).astype(jnp.bfloat16)
    qkv_new = nesterov(gradients[1], qkv_momentum, qkv_weight, qkv_average, rate_qkv)
    out_new = nesterov(gradients[2], out_momentum, out_weight, out_average, rate_out)
    up_new = nesterov(gradients[3], up_momentum, up_weight, up_average, rate_up)
    down_new = nesterov(gradients[4], down_momentum, down_weight, down_average, rate_down)
    norm_new = nesterov(gradients[5], norm_momentum, norm_weight, norm_average, rate_norm)
    return (output, input_grad, qkv_new[0], qkv_new[1], qkv_new[2], out_new[0], out_new[1], out_new[2], up_new[0], up_new[1], up_new[2], down_new[0], down_new[1], down_new[2], norm_new[0], norm_new[1], norm_new[2])
```

```python
import functools
import math

import jax
import jax.numpy as jnp
from jax import lax
from jax.experimental import pallas as pl
from jax.experimental.pallas import tpu as pltpu
from jax.sharding import Mesh, PartitionSpec as P

HEADS = 16
HEAD_DIM = 64
BF = jnp.bfloat16
F32 = jnp.float32
EPS = 1e-05
VMEM_LIMIT = 56 << 20

rate_qkv = 0.04
rate_out = 0.03
rate_up = 0.03
rate_down = 0.02
rate_norm = 0.3

LOG2E = math.log2(math.e)
SCALE = 1.0 / math.sqrt(HEAD_DIM)
NT = (((1,), (1,)), ((), ()))
TN = (((0,), (0,)), ((), ()))


def dot(x, y, dims=None):
    if dims is None:
        return jnp.dot(x, y, preferred_element_type=F32)
    return lax.dot_general(x, y, dims, preferred_element_type=F32)


def call(body, grid, ins, outs, out_shape, args, scratch=(), scalars=0):
    return pl.pallas_call(
        body,
        grid_spec=pltpu.PrefetchScalarGridSpec(
            num_scalar_prefetch=scalars,
            grid=grid,
            in_specs=ins,
            out_specs=outs,
            scratch_shapes=scratch,
        ),
        out_shape=out_shape,
        compiler_params=pltpu.CompilerParams(
            dimension_semantics=("arbitrary",) * len(grid), vmem_limit_bytes=VMEM_LIMIT
        ),
    )(*args)


def shape(rows, cols, dtype):
    return jax.ShapeDtypeStruct((rows, cols), dtype)


def whole(x):
    zeros = (0,) * x.ndim
    return pl.BlockSpec(x.shape, lambda *_: zeros)


def ln_parts(v):
    centre = v - jnp.mean(v, axis=-1, keepdims=True)
    inv = lax.rsqrt(jnp.mean(centre * centre, axis=-1, keepdims=True) + EPS)
    return centre * inv, inv


def ln_grad(xhat, inv, gain, z):
    e = z * gain
    return (
        e - jnp.mean(e, axis=-1, keepdims=True) - xhat * jnp.mean(e * xhat, axis=-1, keepdims=True)
    ) * inv


def column_sums(z, xhat):
    return jnp.concatenate(
        [jnp.sum(z * xhat, axis=0, keepdims=True), jnp.sum(z, axis=0, keepdims=True)], axis=0
    )


def add_to(ref, value):
    @pl.when(pl.program_id(0) == 0)
    def _():
        ref[...] = value

    @pl.when(pl.program_id(0) > 0)
    def _():
        ref[...] += value


def swapped_halves(u):
    lane = lax.broadcasted_iota(jnp.int32, u.shape, 1) % HEAD_DIM
    return jnp.where(lane < HEAD_DIM // 2, pltpu.roll(u, 96, 1), pltpu.roll(u, 32, 1))


def qkv_body(place, x_ref, norm_ref, w_ref, cos_ref, sin_ref, a_ref, q_ref, k_ref, v_ref):
    width = q_ref.shape[1]
    xhat, _ = ln_parts(x_ref[...].astype(F32))
    a = (xhat * norm_ref[0:1, :] + norm_ref[1:2, :]).astype(BF)
    a_ref[...] = a
    cos, sin = cos_ref[...], sin_ref[...]
    for part, ref in enumerate((q_ref, k_ref)):
        rows = dot(a, w_ref[:, part * width : (part + 1) * width])
        for group in range(width // 128):
            u = rows[:, group * 128 : (group + 1) * 128]
            ref[:, group * 128 : (group + 1) * 128] = (u * cos + swapped_halves(u) * sin).astype(BF)
    v_ref[...] = dot(a, w_ref[:, 2 * width :]).astype(BF)


def qkv_forward(place, x_two, norm, w_qkv, cos, sin, span):
    tokens, model = x_two.shape
    width = w_qkv.shape[1] // 3
    row = lambda cols: pl.BlockSpec((span, cols), lambda i, p: (i, 0))
    return call(
        qkv_body,
        (tokens // span,),
        [
            pl.BlockSpec((span, model), lambda i, p: (p[i], 0)),
            whole(norm),
            whole(w_qkv),
            row(128),
            row(128),
        ],
        [row(model), row(width), row(width), row(width)],
        [shape(tokens, model, BF)] + [shape(tokens, width, BF)] * 3,
        (place, x_two, norm, w_qkv, cos, sin),
        scalars=1,
    )


def head_mask(shape_):
    return lax.broadcasted_iota(jnp.int32, shape_, 1) < HEAD_DIM


def forward_body(place, q_ref, k_ref, v_ref, o_ref, lse_ref):
    span = q_ref.shape[0]
    block = pl.program_id(1)
    first = head_mask((span, 128))
    q = q_ref[...]
    zero = jnp.zeros_like(q)
    heads = (jnp.where(first, q, zero), jnp.where(first, zero, q))
    causal = lax.broadcasted_iota(jnp.int32, (span, span), 1) <= lax.broadcasted_iota(
        jnp.int32, (span, span), 0
    )

    def step(start, carry, diagonal):
        k = k_ref[pl.ds(start, span), :]
        v = v_ref[pl.ds(start, span), :]
        result = []
        for head in range(2):
            top, total, acc = carry[head]
            s = dot(heads[head], k, NT) * (SCALE * LOG2E)
            if diagonal:
                s = jnp.where(causal, s, -jnp.inf)
            new_top = jnp.maximum(top, jnp.max(s, axis=1, keepdims=True))
            p = jnp.exp2(s - new_top)
            shrink = jnp.exp2(top - new_top)
            total = total * shrink + jnp.sum(p, axis=1, keepdims=True)
            acc = acc * shrink + dot(p.astype(BF), v)
            result.append((new_top, total, acc))
        return tuple(result)

    empty = (
        jnp.full((span, 1), -1e30, F32),
        jnp.zeros((span, 1), F32),
        jnp.zeros((span, 128), F32),
    )
    carry = step(pl.multiple_of(block * span, span), (empty, empty), True)
    carry = lax.fori_loop(
        0, block, lambda i, c: step(pl.multiple_of(i * span, span), c, False), carry
    )
    (top0, total0, acc0), (top1, total1, acc1) = carry
    o_ref[...] = jnp.where(first, acc0 / total0, acc1 / total1).astype(BF)
    lse = jnp.where(first, top0 + jnp.log2(total0), top1 + jnp.log2(total1))
    turned = lse.T
    lse_ref[...] = jnp.concatenate([turned[0:8], turned[HEAD_DIM : HEAD_DIM + 8]], axis=0)


def attend_forward(place, q, k, v, span):
    tokens, width = q.shape
    pairs, blocks = width // 128, tokens // span
    full = pl.BlockSpec((tokens, 128), lambda h, i, p: (0, h))
    return call(
        forward_body,
        (pairs, blocks),
        [pl.BlockSpec((span, 128), lambda h, i, p: (i, h)), full, full],
        [
            pl.BlockSpec((span, 128), lambda h, i, p: (p[i], h)),
            pl.BlockSpec((16, span), lambda h, i, p: (h, i)),
        ],
        [shape(tokens, width, BF), shape(16 * pairs, tokens, F32)],
        (place, q, k, v),
        scalars=1,
    )


def backward_body(
    place,
    q_ref,
    k_ref,
    v_ref,
    o_ref,
    g_ref,
    lse_ref,
    cos_ref,
    sin_ref,
    dq_ref,
    dk_ref,
    dv_ref,
    dq_acc,
    inner,
    dk_acc,
    dv_acc,
):
    span = dk_ref.shape[0]
    blocks = q_ref.shape[0] // span
    key_block = pl.program_id(1)
    first = head_mask((span, 128))

    @pl.when(key_block == 0)
    def _():
        dq_acc[...] = jnp.zeros_like(dq_acc)
        for i in range(blocks):
            rows = pl.ds(pl.multiple_of(place[i] * span, span), span)
            prod = (o_ref[rows, :].astype(F32) * g_ref[rows, :].astype(F32)).T
            for head in range(2):
                inner[head * 8 : head * 8 + 1, i * span : (i + 1) * span] = jnp.sum(
                    prod[head * HEAD_DIM : (head + 1) * HEAD_DIM], axis=0, keepdims=True
                )

    dk_acc[...] = jnp.zeros_like(dk_acc)
    dv_acc[...] = jnp.zeros_like(dv_acc)
    k = k_ref[...]
    v = v_ref[...]
    zero = jnp.zeros_like(k)
    keys = (jnp.where(first, k, zero), jnp.where(first, zero, k))
    values = (jnp.where(first, v, zero), jnp.where(first, zero, v))
    causal = lax.broadcasted_iota(jnp.int32, (span, span), 0) <= lax.broadcasted_iota(
        jnp.int32, (span, span), 1
    )

    def step(block, diagonal):
        start = pl.multiple_of(block * span, span)
        q = q_ref[pl.ds(start, span), :]
        g = g_ref[pl.ds(pl.multiple_of(place[block] * span, span), span), :]
        for head in range(2):
            mine = first if head == 0 else jnp.logical_not(first)
            lse = lse_ref[head * 8 : head * 8 + 1, pl.ds(start, span)]
            mean = inner[head * 8 : head * 8 + 1, pl.ds(start, span)]
            s = dot(keys[head], q, NT) * (SCALE * LOG2E)
            p = jnp.exp2(s - lse)
            if diagonal:
                p = jnp.where(causal, p, 0.0)
            dp = dot(values[head], g, NT)
            ds = (p * (dp - mean)).astype(BF)
            dv_acc[...] += dot(p.astype(BF), jnp.where(mine, g, zero))
            dk_acc[...] += dot(ds, jnp.where(mine, q, zero))
            dq_acc[pl.ds(start, span), :] += dot(ds, keys[head], TN)

    step(key_block, True)

    @pl.loop(key_block + 1, blocks)
    def _(block):
        step(block, False)

    start = pl.multiple_of(key_block * span, span)
    cos, sin = cos_ref[pl.ds(start, span), :], sin_ref[pl.ds(start, span), :]
    dk = dk_acc[...] * SCALE
    dk_ref[...] = (dk * cos - swapped_halves(dk) * sin).astype(BF)
    dv_ref[...] = dv_acc[...].astype(BF)
    dq = dq_acc[pl.ds(start, span), :] * SCALE
    dq_ref[...] = (dq * cos - swapped_halves(dq) * sin).astype(BF)


def attend_backward(place, q, k, v, o, g, lse, cos, sin, span):
    tokens, width = q.shape
    pairs, blocks = width // 128, tokens // span
    full = pl.BlockSpec((tokens, 128), lambda h, i, p: (0, h))
    part = pl.BlockSpec((span, 128), lambda h, i, p: (i, h))
    return call(
        backward_body,
        (pairs, blocks),
        [
            full,
            part,
            part,
            full,
            full,
            pl.BlockSpec((16, tokens), lambda h, i, p: (h, 0)),
            whole(cos),
            whole(sin),
        ],
        [part, part, part],
        [shape(tokens, width, BF)] * 3,
        (place, q, k, v, o, g, lse, cos, sin),
        scratch=[
            pltpu.VMEM((tokens, 128), F32),
            pltpu.VMEM((16, tokens), F32),
            pltpu.VMEM((span, 128), F32),
            pltpu.VMEM((span, 128), F32),
        ],
        scalars=1,
    )


def project_body(om_ref, oo_ref, wm_ref, wo_ref, x_ref, norm_ref, a_ref, h_ref, c_ref):
    a = dot(om_ref[...], wm_ref[...]) + dot(oo_ref[...], wo_ref[...])
    a_ref[...] = a
    xhat, _ = ln_parts(a)
    h = x_ref[...].astype(F32) + (xhat * norm_ref[2:3, :] + norm_ref[3:4, :])
    h_ref[...] = h
    hhat, _ = ln_parts(h)
    c_ref[...] = (hhat * norm_ref[4:5, :] + norm_ref[5:6, :]).astype(BF)


def project(o_mine, o_other, w_mine, w_other, x, norm, rows=256):
    tokens, model = x.shape
    row = lambda cols: pl.BlockSpec((rows, cols), lambda i: (i, 0))
    half = o_mine.shape[1]
    return call(
        project_body,
        (tokens // rows,),
        [row(half), row(half), whole(w_mine), whole(w_other), row(model), whole(norm)],
        [row(model)] * 3,
        [shape(tokens, model, F32), shape(tokens, model, F32), shape(tokens, model, BF)],
        (o_mine, o_other, w_mine, w_other, x, norm),
    )


def turn_body(m_ref, r_ref, h_ref, y_ref, norm_ref, out_ref, dm_ref, sums_ref):
    xhat, inv = ln_parts(m_ref[...] + r_ref[...].astype(F32))
    gain = norm_ref[6:7, :]
    out_ref[...] = (h_ref[...] + (xhat * gain + norm_ref[7:8, :])).astype(BF)
    z = y_ref[...].astype(F32)
    dm_ref[...] = ln_grad(xhat, inv, gain, z).astype(BF)
    add_to(sums_ref, column_sums(z, xhat))


def turn(m_part, m_other, h, y, norm, rows=256):
    tokens, model = y.shape
    row = pl.BlockSpec((rows, model), lambda i: (i, 0))
    return call(
        turn_body,
        (tokens // rows,),
        [row, row, row, row, whole(norm)],
        [row, row, pl.BlockSpec((2, model), lambda i: (0, 0))],
        [shape(tokens, model, BF), shape(tokens, model, BF), shape(2, model, F32)],
        (m_part, m_other, h, y, norm),
    )


def descend_body(
    dc_ref, r_ref, h_ref, a_ref, y_ref, norm_ref, dh_ref, da_ref, sums3_ref, sums2_ref
):
    dc = dc_ref[...] + r_ref[...].astype(F32)
    hhat, inv = ln_parts(h_ref[...])
    dh = y_ref[...].astype(F32) + ln_grad(hhat, inv, norm_ref[4:5, :], dc)
    dh_ref[...] = dh
    add_to(sums3_ref, column_sums(dc, hhat))
    ahat, inv = ln_parts(a_ref[...])
    da_ref[...] = ln_grad(ahat, inv, norm_ref[2:3, :], dh).astype(BF)
    add_to(sums2_ref, column_sums(dh, ahat))


def descend(dc_part, dc_other, h, a, y, norm, rows=256):
    tokens, model = y.shape
    row = pl.BlockSpec((rows, model), lambda i: (i, 0))
    sums = pl.BlockSpec((2, model), lambda i: (0, 0))
    return call(
        descend_body,
        (tokens // rows,),
        [row] * 5 + [whole(norm)],
        [row, row, sums, sums],
        [
            shape(tokens, model, F32),
            shape(tokens, model, BF),
            shape(2, model, F32),
            shape(2, model, F32),
        ],
        (dc_part, dc_other, h, a, y, norm),
    )


def up_down_body(c_ref, wu_ref, wd_ref, g_ref, s_ref, m_ref, acc):
    u = dot(c_ref[...], wu_ref[...])
    k = math.sqrt(2.0 / math.pi)
    square = u * u
    t = jnp.tanh(u * (k + (k * 0.044715) * square))
    half = 0.5 + 0.5 * t
    g = (u * half).astype(BF)
    g_ref[...] = g
    s_ref[...] = (
        half + (0.5 * u) * (1.0 - t * t) * (k + (3.0 * k * 0.044715) * square)
    ).astype(BF)
    add_to(acc, dot(g, wd_ref[...]))

    @pl.when(pl.program_id(0) == pl.num_programs(0) - 1)
    def _():
        m_ref[...] = acc[...].astype(m_ref.dtype)


def up_down(c, w_up, w_down, dtype, cols=512):
    tokens, model = c.shape
    units = w_up.shape[1]
    wide = pl.BlockSpec((tokens, cols), lambda i: (0, i))
    return call(
        up_down_body,
        (units // cols,),
        [
            whole(c),
            pl.BlockSpec((model, cols), lambda i: (0, i)),
            pl.BlockSpec((cols, model), lambda i: (i, 0)),
        ],
        [wide, wide, pl.BlockSpec((tokens, model), lambda i: (0, 0))],
        [shape(tokens, units, BF), shape(tokens, units, BF), shape(tokens, model, dtype)],
        (c, w_up, w_down),
        scratch=[pltpu.VMEM((tokens, model), F32)],
    )


def down_up_body(dm_ref, s_ref, wu_ref, wd_ref, du_ref, dc_ref, acc):
    du = (dot(dm_ref[...], wd_ref[...], NT) * s_ref[...].astype(F32)).astype(BF)
    du_ref[...] = du
    add_to(acc, dot(du, wu_ref[...], NT))

    @pl.when(pl.program_id(0) == pl.num_programs(0) - 1)
    def _():
        dc_ref[...] = acc[...].astype(dc_ref.dtype)


def down_up(dm, slope, w_up, w_down, dtype, cols=512):
    tokens, model = dm.shape
    units = w_up.shape[1]
    wide = pl.BlockSpec((tokens, cols), lambda i: (0, i))
    return call(
        down_up_body,
        (units // cols,),
        [
            whole(dm),
            wide,
            pl.BlockSpec((model, cols), lambda i: (0, i)),
            pl.BlockSpec((cols, model), lambda i: (i, 0)),
        ],
        [wide, pl.BlockSpec((tokens, model), lambda i: (0, 0))],
        [shape(tokens, units, BF), shape(tokens, model, dtype)],
        (dm, slope, w_up, w_down),
        scratch=[pltpu.VMEM((tokens, model), F32)],
    )


def input_part(q_ref, k_ref, v_ref, w_ref):
    width = q_ref.shape[1]
    return (
        dot(q_ref[...], w_ref[:, :width], NT)
        + dot(k_ref[...], w_ref[:, width : 2 * width], NT)
        + dot(v_ref[...], w_ref[:, 2 * width :], NT)
    )


def other_body(inverse, q_ref, k_ref, v_ref, w_ref, out_ref):
    out_ref[...] = input_part(q_ref, k_ref, v_ref, w_ref).astype(BF)


def own_body(
    inverse, q_ref, k_ref, v_ref, w_ref, r_ref, x_ref, dh_ref, norm_ref, out_ref, sums_ref
):
    z = input_part(q_ref, k_ref, v_ref, w_ref) + r_ref[...].astype(F32)
    xhat, inv = ln_parts(x_ref[...].astype(F32))
    out_ref[...] = (dh_ref[...] + ln_grad(xhat, inv, norm_ref[0:1, :], z)).astype(BF)
    add_to(sums_ref, column_sums(z, xhat))


def input_other(inverse, dq, dk, dv, w_qkv, span):
    width, model = dq.shape[1], w_qkv.shape[0]
    part = pl.BlockSpec((span, width), lambda i, p: (p[i + 2], 0))
    return call(
        other_body,
        (2,),
        [part, part, part, whole(w_qkv)],
        pl.BlockSpec((span, model), lambda i, p: (i, 0)),
        shape(2 * span, model, BF),
        (inverse, dq, dk, dv, w_qkv),
        scalars=1,
    )


def input_own(inverse, dq, dk, dv, w_qkv, recv, x, dh, norm, span):
    width, model = dq.shape[1], w_qkv.shape[0]
    part = pl.BlockSpec((span, width), lambda i, p: (p[i], 0))
    row = pl.BlockSpec((span, model), lambda i, p: (i, 0))
    return call(
        own_body,
        (2,),
        [part, part, part, whole(w_qkv), row, row, row, whole(norm)],
        [row, pl.BlockSpec((2, model), lambda i, p: (0, 0))],
        [shape(2 * span, model, BF), shape(2, model, F32)],
        (inverse, dq, dk, dv, w_qkv, recv, x, dh, norm),
        scalars=1,
    )


def nesterov(gradient, momentum, weight, average, step_rate, token_total):
    scaled = gradient / token_total
    new_momentum = 0.5 * momentum + scaled
    new_weight = weight - step_rate * math.sqrt(token_total) * (scaled + 0.5 * new_momentum)
    new_average = 0.5 * average + 0.5 * new_weight
    return (new_momentum, new_weight, new_average)


def per_device(
    tokens,
    cotangent,
    pair_order,
    qkv_weight,
    qkv_momentum,
    qkv_average,
    out_weight,
    out_momentum,
    out_average,
    up_weight,
    up_momentum,
    up_average,
    down_weight,
    down_momentum,
    down_average,
    norm_weight,
    norm_momentum,
    norm_average,
):
    chips = lax.axis_size("chip")
    ctx_count = lax.axis_size("ctx")
    assert ctx_count == 2 and pair_order.shape[0] == 1 and chips & (chips - 1) == 0
    levels = chips.bit_length() - 1
    chip, core, side = lax.axis_index("chip"), lax.axis_index("core"), lax.axis_index("ctx")
    count, model = tokens.shape
    span = count // 2
    token_total = count * chips * 4
    half = model // 2
    everyone = ("chip", "ctx")
    flip = [(0, 1), (1, 0)]

    def to_core(x):
        return lax.ppermute(x, "core", flip)

    def regroup(x):
        return lax.ppermute(x, ("core", "ctx"), [(0, 0), (1, 2), (2, 1), (3, 3)])

    def exchange(x, level):
        if level == "ctx":
            return lax.ppermute(x, "ctx", flip)
        return lax.ppermute(x, "chip", [(i, i ^ (1 << level)) for i in range(chips)])

    def pick(x, index, dim):
        return lax.dynamic_index_in_dim(x, index, dim, keepdims=False)

    def by_core(mine, other):
        return jnp.where(core == 0, jnp.stack([mine, other]), jnp.stack([other, mine]))

    def reduce_rows(g, order):
        rest = g.shape[levels:]
        names = [levels - 1 - i for i in range(levels)] + ["ctx"]
        if len(rest) == 4:
            names = names[:-1] + ["core", "ctx"]
        for index, level in enumerate(order):
            dim = names.index(level)
            bit = side if level == "ctx" else (chip >> level) & 1
            sent = exchange(pick(g, 1 - bit, dim), level)
            g = pick(g, bit, dim).astype(F32) + sent.astype(F32)
            if index < len(order) - 1:
                g = g.astype(BF)
            names.pop(dim)
        return g

    cube = (2,) * levels
    order_a = [0, "ctx"] + list(range(1, levels))
    order_b = ["ctx", 0] + list(range(1, levels))

    w = qkv_weight.astype(BF).reshape(-1, 3, HEADS // 2, 2, HEAD_DIM)
    mine, other = pick(w, core, 3), to_core(pick(w, 1 - core, 3))
    rows = w.shape[0]
    local = by_core(mine.reshape(rows, -1), other.reshape(rows, -1)).reshape(2 * rows, -1)
    w_qkv = lax.all_gather(local, everyone, axis=0, tiled=True)
    w_qkv = (
        w_qkv.reshape(chips, 2, 2, rows, 3 * half).transpose(0, 2, 1, 3, 4).reshape(model, 3 * half)
    )
    w_out = lax.all_gather(out_weight.astype(BF), everyone, axis=0, tiled=True)
    w_out_other = to_core(w_out)
    units = down_weight.shape[0]
    w = up_weight.astype(BF).reshape(rows, chips, 2, 2 * units)
    mine, other = pick(w, core, 2), to_core(pick(w, 1 - core, 2))
    local = by_core(mine.reshape(rows, -1), other.reshape(rows, -1)).reshape(2 * rows, -1)
    w_up = lax.all_gather(local, everyone, axis=0, tiled=True)
    w_up = w_up.reshape(chips, 2, 2, rows, -1).transpose(0, 2, 1, 3, 4).reshape(model, -1)
    w_down = lax.all_gather(down_weight.astype(BF), everyone, axis=0, tiled=True)
    norm = lax.all_gather(norm_weight.astype(BF), ("chip", "core", "ctx"), axis=1, tiled=True).astype(F32)

    x = regroup(tokens)
    y = regroup(cotangent)
    x_two = jnp.concatenate([x, to_core(x)], axis=0)
    order_row = jnp.where(core == side, pair_order, to_core(pair_order))[0]
    mine_first = pick(order_row, core, 0) == 0
    place = jnp.where(
        mine_first, jnp.array([0, 2, 3, 1], jnp.int32), jnp.array([2, 0, 1, 3], jnp.int32)
    )
    inverse = jnp.where(
        mine_first, jnp.array([0, 3, 1, 2], jnp.int32), jnp.array([1, 2, 0, 3], jnp.int32)
    )
    steps = jnp.arange(HEAD_DIM // 2, dtype=F32)
    frequency = jnp.exp(steps * (-math.log(10000.0) / (HEAD_DIM // 2)))
    angles = jnp.arange(2 * count, dtype=jnp.int32).astype(F32)[:, None] * frequency[None, :]
    cos, sin = jnp.cos(angles), jnp.sin(angles)
    cos_table = jnp.concatenate([cos] * 4, axis=1)
    sin_table = jnp.concatenate([-sin, sin] * 2, axis=1)

    a, q, k, v = qkv_forward(place, x_two, norm, w_qkv, cos_table, sin_table, span)
    o, lse = attend_forward(place, q, k, v, span)
    o_mine, o_sent = o[:count], o[count:]
    o_other = to_core(o_sent)
    projected, hidden, c = project(o_mine, o_other, w_out, w_out_other, x, norm)
    c_other = to_core(c)
    g_other, slope_other, m_sent = up_down(c_other, w_up, w_down, BF)
    m_recv = to_core(m_sent)
    g_mine, slope_mine, m_part = up_down(c, w_up, w_down, F32)
    output, dm, sums4 = turn(m_part, m_recv, hidden, y, norm)

    dm_other = to_core(dm)
    du_mine, dc_part = down_up(dm, slope_mine, w_up, w_down, F32)
    du_other, dc_sent = down_up(dm_other, slope_other, w_up, w_down, BF)
    dc_recv = to_core(dc_sent)
    g_two = jnp.concatenate([g_mine, g_other], axis=0)
    dm_two = jnp.concatenate([dm, dm_other], axis=0)
    grad_down = dot(g_two, dm_two, TN).astype(BF)
    c_two = jnp.concatenate([c, c_other], axis=0)
    du_two = jnp.concatenate([du_mine, du_other], axis=0)
    grad_up = dot(c_two, du_two, TN).astype(BF)
    dh, da, sums3, sums2 = descend(dc_part, dc_recv, hidden, projected, y, norm)
    da_two = jnp.concatenate([da, to_core(da)], axis=0)
    do = dot(da_two, w_out, NT).astype(BF)
    grad_out = dot(o, da_two, TN).astype(BF)
    dq, dk, dv = attend_backward(place, q, k, v, o, do, lse, cos_table, sin_table, span)
    dx_recv = to_core(input_other(inverse, dq, dk, dv, w_qkv, span))
    grad_q, grad_k, grad_v = (dot(a, d, TN).astype(BF) for d in (dq, dk, dv))
    input_grad, sums1 = input_own(inverse, dq, dk, dv, w_qkv, dx_recv, x, dh, norm, span)

    down_sum = jnp.concatenate(
        [
            reduce_rows(grad_down[:, s].reshape(*cube, 2, units, half), o_)
            for s, o_ in ((slice(0, half), order_a), (slice(half, model), order_b))
        ],
        axis=-1,
    ).reshape(units, model)
    out_sum = jnp.concatenate(
        [
            reduce_rows(grad_out[:, s].reshape(*cube, 2, rows, half), o_)
            for s, o_ in ((slice(0, half), order_a), (slice(half, model), order_b))
        ],
        axis=-1,
    ).reshape(rows, model)

    def from_cores(part):
        return by_core(pick(part, core, 0), to_core(pick(part, 1 - core, 0)))

    ff_half = grad_up.shape[1] // 2
    up_part = jnp.concatenate(
        [
            reduce_rows(grad_up[:, s].reshape(*cube, 2, 2, rows, ff_half), o_)
            for s, o_ in ((slice(0, ff_half), order_a), (slice(ff_half, 2 * ff_half), order_b))
        ],
        axis=-1,
    )
    up_sum = (
        from_cores(up_part)
        .reshape(2, rows, chips, 2 * units)
        .transpose(1, 2, 0, 3)
        .reshape(rows, 4 * chips * units)
    )
    qkv_part = jnp.stack(
        [
            reduce_rows(g.reshape(*cube, 2, 2, rows, half), o_)
            for g, o_ in ((grad_q, order_a), (grad_k, order_b), (grad_v, order_a))
        ],
        axis=2,
    )
    qkv_sum = (
        from_cores(qkv_part)
        .reshape(2, rows, 3, HEADS // 2, HEAD_DIM)
        .transpose(1, 2, 3, 0, 4)
        .reshape(rows, 3 * model)
    )
    norm_grad = jnp.concatenate([sums1, sums2, sums3, sums4], axis=0)
    norm_grad = norm_grad + to_core(norm_grad)
    tiles = norm_grad.reshape(8, *cube, 2, 2, rows)
    tiles = jnp.moveaxis(tiles, 0, levels + 2)
    tiles = pick(tiles, core, levels)
    norm_sum = reduce_rows_f32(tiles, order_a, levels, chip, side, exchange, pick)

    qkv_new = nesterov(qkv_sum, qkv_momentum, qkv_weight, qkv_average, rate_qkv, token_total)
    out_new = nesterov(out_sum, out_momentum, out_weight, out_average, rate_out, token_total)
    up_new = nesterov(up_sum, up_momentum, up_weight, up_average, rate_up, token_total)
    down_new = nesterov(down_sum, down_momentum, down_weight, down_average, rate_down, token_total)
    norm_new = nesterov(norm_sum, norm_momentum, norm_weight, norm_average, rate_norm, token_total)
    return (
        regroup(output),
        regroup(input_grad),
        *qkv_new,
        *out_new,
        *up_new,
        *down_new,
        *norm_new,
    )


def reduce_rows_f32(g, order, levels, chip, side, exchange, pick):
    names = [levels - 1 - i for i in range(levels)] + ["ctx"]
    for level in order:
        dim = names.index(level)
        bit = side if level == "ctx" else (chip >> level) & 1
        g = pick(g, bit, dim) + exchange(pick(g, 1 - bit, dim), level)
        names.pop(dim)
    return g


def solution(mesh):
    dp, ctx = mesh.shape["dp"], mesh.shape["ctx"]
    inner = Mesh(mesh.devices.reshape(dp // 2, 2, ctx), ("chip", "core", "ctx"))
    rows = P(("chip", "core", "ctx"), None)
    cols = P(None, ("chip", "core", "ctx"))
    return jax.shard_map(
        per_device,
        mesh=inner,
        in_specs=(rows, rows, P(("chip", "core"), None)) + (rows,) * 12 + (cols,) * 3,
        out_specs=(rows,) * 14 + (cols,) * 3,
        check_vma=False,
    )
```

```python
import functools
import math

import jax
import jax.numpy as jnp
from jax import lax
from jax.experimental import pallas as pl
from jax.experimental.pallas import tpu as pltpu
from jax.sharding import Mesh, PartitionSpec as P

HEADS = 16
HEAD_DIM = 64
BF = jnp.bfloat16
F32 = jnp.float32
EPS = 1e-05
VMEM_LIMIT = 56 << 20

rate_qkv = 0.04
rate_out = 0.03
rate_up = 0.03
rate_down = 0.02
rate_norm = 0.3

LOG2E = math.log2(math.e)
SCALE = 1.0 / math.sqrt(HEAD_DIM)
NT = (((1,), (1,)), ((), ()))
TN = (((0,), (0,)), ((), ()))


def dot(x, y, dims=None):
    if dims is None:
        return jnp.dot(x, y, preferred_element_type=F32)
    return lax.dot_general(x, y, dims, preferred_element_type=F32)


def call(body, grid, ins, outs, out_shape, args, scratch=(), scalars=0):
    return pl.pallas_call(
        body,
        grid_spec=pltpu.PrefetchScalarGridSpec(
            num_scalar_prefetch=scalars,
            grid=grid,
            in_specs=ins,
            out_specs=outs,
            scratch_shapes=scratch,
        ),
        out_shape=out_shape,
        compiler_params=pltpu.CompilerParams(
            dimension_semantics=("arbitrary",) * len(grid), vmem_limit_bytes=VMEM_LIMIT
        ),
    )(*args)


def shape(rows, cols, dtype):
    return jax.ShapeDtypeStruct((rows, cols), dtype)


def whole(x):
    zeros = (0,) * x.ndim
    return pl.BlockSpec(x.shape, lambda *_: zeros)


def ln_parts(v):
    centre = v - jnp.mean(v, axis=-1, keepdims=True)
    inv = lax.rsqrt(jnp.mean(centre * centre, axis=-1, keepdims=True) + EPS)
    return centre * inv, inv


def ln_grad(xhat, inv, gain, z):
    e = z * gain
    return (
        e - jnp.mean(e, axis=-1, keepdims=True) - xhat * jnp.mean(e * xhat, axis=-1, keepdims=True)
    ) * inv


def column_sums(z, xhat):
    return jnp.concatenate(
        [jnp.sum(z * xhat, axis=0, keepdims=True), jnp.sum(z, axis=0, keepdims=True)], axis=0
    )


def add_to(ref, value):
    @pl.when(pl.program_id(0) == 0)
    def _():
        ref[...] = value

    @pl.when(pl.program_id(0) > 0)
    def _():
        ref[...] += value


def regroup_lanes(u, size):
    lane = lax.broadcasted_iota(jnp.int32, (u.shape[0], 128), 1) % (4 * size)
    groups = []
    for start in range(0, u.shape[1], 128):
        w = u[:, start : start + 128]
        w = jnp.where(
            (lane >= size) & (lane < 2 * size),
            pltpu.roll(w, 128 - size, 1),
            jnp.where((lane >= 2 * size) & (lane < 3 * size), pltpu.roll(w, size, 1), w),
        )
        groups.append(w)
    return jnp.concatenate(groups, axis=1)


def swapped_halves(u):
    lane = lax.broadcasted_iota(jnp.int32, u.shape, 1) % HEAD_DIM
    return jnp.where(lane < HEAD_DIM // 2, pltpu.roll(u, 96, 1), pltpu.roll(u, 32, 1))


def qkv_rows(a, w, cos, sin, q_ref, k_ref, v_ref):
    width = q_ref.shape[1]
    for part, ref in enumerate((q_ref, k_ref)):
        rows = dot(a, w[:, part * width : (part + 1) * width])
        for group in range(width // 128):
            u = rows[:, group * 128 : (group + 1) * 128]
            ref[:, group * 128 : (group + 1) * 128] = (u * cos + swapped_halves(u) * sin).astype(BF)
    v_ref[...] = dot(a, w[:, 2 * width :]).astype(BF)


def first_qkv_body(
    size,
    inverse,
    own_ref,
    other_ref,
    w_ref,
    cos_ref,
    sin_ref,
    a_ref,
    q_ref,
    k_ref,
    v_ref,
):
    owners = w_ref.shape[0]
    x = jnp.where(pl.program_id(0) < 2, own_ref[...], other_ref[...])
    xhat, _ = ln_parts(x.astype(F32))
    norm = jnp.concatenate(
        [w_ref[n, 2 * size : 2 * size + 8, : 2 * size] for n in range(owners)], axis=1
    ).astype(F32)
    a = (regroup_lanes(xhat, size) * norm[0:1, :] + norm[1:2, :]).astype(BF)
    a_ref[...] = a
    w = w_ref[:, : 2 * size, :].reshape(2 * size * owners, w_ref.shape[2])
    qkv_rows(a, w, cos_ref[...], sin_ref[...], q_ref, k_ref, v_ref)


def next_qkv_body(a_ref, w_ref, cos_ref, sin_ref, q_ref, k_ref, v_ref):
    qkv_rows(a_ref[...], w_ref[...], cos_ref[...], sin_ref[...], q_ref, k_ref, v_ref)


def first_qkv(size, inverse, own, other, w_qkv, cos, sin, span):
    tokens, model = 2 * own.shape[0], own.shape[1]
    width = w_qkv.shape[2] // 3
    row = lambda cols: pl.BlockSpec((span, cols), lambda i, p: (p[i], 0))
    return call(
        functools.partial(first_qkv_body, size),
        (tokens // span,),
        [
            pl.BlockSpec((span, model), lambda i, p: (jnp.minimum(i, 1), 0)),
            pl.BlockSpec((span, model), lambda i, p: (jnp.maximum(i - 2, 0), 0)),
            whole(w_qkv),
            row(128),
            row(128),
        ],
        [row(model), row(width), row(width), row(width)],
        [shape(tokens, model, BF)] + [shape(tokens, width, BF)] * 3,
        (inverse, own, other, w_qkv, cos, sin),
        scalars=1,
    )


def next_qkv(a, w_qkv, cos, sin, span):
    tokens, model = a.shape
    width = w_qkv.shape[1] // 3
    row = lambda cols: pl.BlockSpec((span, cols), lambda i: (i, 0))
    return call(
        next_qkv_body,
        (tokens // span,),
        [row(model), whole(w_qkv), row(128), row(128)],
        [row(width)] * 3,
        [shape(tokens, width, BF)] * 3,
        (a, w_qkv, cos, sin),
    )


def head_mask(shape_):
    return lax.broadcasted_iota(jnp.int32, shape_, 1) < HEAD_DIM


def forward_body(inverse, q_ref, k_ref, v_ref, own_ref, sent_ref, lse_ref):
    span = q_ref.shape[0]
    turn_index = pl.program_id(1)
    block = inverse[turn_index]
    first = head_mask((span, 128))
    q = q_ref[...]
    zero = jnp.zeros_like(q)
    heads = (jnp.where(first, q, zero), jnp.where(first, zero, q))
    causal = lax.broadcasted_iota(jnp.int32, (span, span), 1) <= lax.broadcasted_iota(
        jnp.int32, (span, span), 0
    )

    def step(start, carry, diagonal):
        k = k_ref[pl.ds(start, span), :]
        v = v_ref[pl.ds(start, span), :]
        result = []
        for head in range(2):
            top, total, acc = carry[head]
            s = dot(heads[head], k, NT) * (SCALE * LOG2E)
            if diagonal:
                s = jnp.where(causal, s, -jnp.inf)
            new_top = jnp.maximum(top, jnp.max(s, axis=1, keepdims=True))
            p = jnp.exp2(s - new_top)
            shrink = jnp.exp2(top - new_top)
            total = total * shrink + jnp.sum(p, axis=1, keepdims=True)
            acc = acc * shrink + dot(p.astype(BF), v)
            result.append((new_top, total, acc))
        return tuple(result)

    empty = (
        jnp.full((span, 1), -1e30, F32),
        jnp.zeros((span, 1), F32),
        jnp.zeros((span, 128), F32),
    )
    carry = step(pl.multiple_of(block * span, span), (empty, empty), True)
    carry = lax.fori_loop(
        0, block, lambda i, c: step(pl.multiple_of(i * span, span), c, False), carry
    )
    (top0, total0, acc0), (top1, total1, acc1) = carry
    o = jnp.where(first, acc0 / total0, acc1 / total1).astype(BF)

    @pl.when(turn_index < 2)
    def _():
        own_ref[...] = o

    @pl.when(turn_index >= 2)
    def _():
        sent_ref[...] = o

    lse = jnp.where(first, top0 + jnp.log2(total0), top1 + jnp.log2(total1))
    turned = lse.T
    lse_ref[...] = jnp.concatenate([turned[0:8], turned[HEAD_DIM : HEAD_DIM + 8]], axis=0)


def attend_forward(inverse, q, k, v, span):
    tokens, width = q.shape
    pairs, blocks = width // 128, tokens // span
    full = pl.BlockSpec((tokens, 128), lambda h, i, p: (0, h))
    return call(
        forward_body,
        (pairs, blocks),
        [pl.BlockSpec((span, 128), lambda h, i, p: (p[i], h)), full, full],
        [
            pl.BlockSpec((span, 128), lambda h, i, p: (jnp.minimum(i, 1), h)),
            pl.BlockSpec((span, 128), lambda h, i, p: (jnp.maximum(i - 2, 0), h)),
            pl.BlockSpec((16, span), lambda h, i, p: (h, p[i])),
        ],
        [
            shape(tokens // 2, width, BF),
            shape(tokens // 2, width, BF),
            shape(16 * pairs, tokens, F32),
        ],
        (inverse, q, k, v),
        scalars=1,
    )


def backward_body(
    inverse,
    q_ref,
    k_ref,
    v_ref,
    own_ref,
    sent_ref,
    g_ref,
    lse_ref,
    cos_ref,
    sin_ref,
    dq_ref,
    dk_ref,
    dv_ref,
    dq_acc,
    inner,
    dk_acc,
    dv_acc,
):
    span = dk_ref.shape[0]
    blocks = q_ref.shape[0] // span
    key_block = pl.program_id(0)
    first = head_mask((span, 128))

    @pl.when(key_block == 0)
    def _():
        dq_acc[...] = jnp.zeros_like(dq_acc)
        for i in range(blocks):
            o_ref = own_ref if i < 2 else sent_ref
            start = pl.multiple_of(inverse[i] * span, span)
            o = o_ref[(i % 2) * span : (i % 2 + 1) * span, :].astype(F32)
            prod = (o * g_ref[pl.ds(start, span), :].astype(F32)).T
            for head in range(2):
                inner[head * 8 : head * 8 + 1, pl.ds(start, span)] = jnp.sum(
                    prod[head * HEAD_DIM : (head + 1) * HEAD_DIM], axis=0, keepdims=True
                )

    dk_acc[...] = jnp.zeros_like(dk_acc)
    dv_acc[...] = jnp.zeros_like(dv_acc)
    k = k_ref[...]
    v = v_ref[...]
    zero = jnp.zeros_like(k)
    keys = (jnp.where(first, k, zero), jnp.where(first, zero, k))
    values = (jnp.where(first, v, zero), jnp.where(first, zero, v))
    causal = lax.broadcasted_iota(jnp.int32, (span, span), 0) <= lax.broadcasted_iota(
        jnp.int32, (span, span), 1
    )

    def step(block, diagonal):
        start = pl.multiple_of(block * span, span)
        q = q_ref[pl.ds(start, span), :]
        g = g_ref[pl.ds(start, span), :]
        for head in range(2):
            mine = first if head == 0 else jnp.logical_not(first)
            lse = lse_ref[head * 8 : head * 8 + 1, pl.ds(start, span)]
            mean = inner[head * 8 : head * 8 + 1, pl.ds(start, span)]
            s = dot(keys[head], q, NT) * (SCALE * LOG2E)
            p = jnp.exp2(s - lse)
            if diagonal:
                p = jnp.where(causal, p, 0.0)
            dp = dot(values[head], g, NT)
            ds = (p * (dp - mean)).astype(BF)
            dv_acc[...] += dot(p.astype(BF), jnp.where(mine, g, zero))
            dk_acc[...] += dot(ds, jnp.where(mine, q, zero))
            dq_acc[pl.ds(start, span), :] += dot(ds, keys[head], TN)

    step(key_block, True)

    @pl.loop(key_block + 1, blocks)
    def _(block):
        step(block, False)

    start = pl.multiple_of(key_block * span, span)
    cos, sin = cos_ref[pl.ds(start, span), :], sin_ref[pl.ds(start, span), :]
    dk = dk_acc[...] * SCALE
    dk_ref[...] = (dk * cos - swapped_halves(dk) * sin).astype(BF)
    dv_ref[...] = dv_acc[...].astype(BF)
    dq = dq_acc[pl.ds(start, span), :] * SCALE
    dq_ref[...] = (dq * cos - swapped_halves(dq) * sin).astype(BF)


def attend_backward(inverse, q, k, v, own, sent, g, lse, cos, sin, span, pair, g_pair):
    tokens = q.shape[0]
    blocks = tokens // span
    full = pl.BlockSpec((tokens, 128), lambda i, p: (0, pair))
    part = pl.BlockSpec((span, 128), lambda i, p: (i, pair))
    side = pl.BlockSpec((tokens // 2, 128), lambda i, p: (0, pair))
    out = pl.BlockSpec((span, 128), lambda i, p: (i, 0))
    return call(
        backward_body,
        (blocks,),
        [
            full,
            part,
            part,
            side,
            side,
            pl.BlockSpec((tokens, 128), lambda i, p: (0, g_pair)),
            pl.BlockSpec((16, tokens), lambda i, p: (pair, 0)),
            whole(cos),
            whole(sin),
        ],
        [out, out, out],
        [shape(tokens, 128, BF)] * 3,
        (inverse, q, k, v, own, sent, g, lse, cos, sin),
        scratch=[
            pltpu.VMEM((tokens, 128), F32),
            pltpu.VMEM((16, tokens), F32),
            pltpu.VMEM((span, 128), F32),
            pltpu.VMEM((span, 128), F32),
        ],
        scalars=1,
    )


def mix_body(inverse, own_ref, other_ref, w_ref, out_ref):
    index = pl.program_id(0)

    @pl.when(index < 2)
    def _():
        out_ref[...] = dot(own_ref[...], w_ref[...], NT).astype(BF)

    @pl.when(index >= 2)
    def _():
        out_ref[...] = dot(other_ref[...], w_ref[...], NT).astype(BF)


def mix_gradient(inverse, own, other, w_out, span):
    model = own.shape[1]
    width = w_out.shape[0]
    return call(
        mix_body,
        (4,),
        [
            pl.BlockSpec((span, model), lambda i, p: (jnp.minimum(i, 1), 0)),
            pl.BlockSpec((span, model), lambda i, p: (jnp.maximum(i - 2, 0), 0)),
            whole(w_out),
        ],
        pl.BlockSpec((span, width), lambda i, p: (p[i], 0)),
        shape(4 * span, width, BF),
        (inverse, own, other, w_out),
        scalars=1,
    )


def project_body(
    size, m0_ref, m1_ref, o0_ref, o1_ref, wm_ref, wo_ref, x_ref, norm_ref, a_ref, h_ref, c_ref
):
    half = m0_ref.shape[1]
    a = (
        dot(m0_ref[...], wm_ref[:half, :])
        + dot(m1_ref[...], wm_ref[half:, :])
        + dot(o0_ref[...], wo_ref[:half, :])
        + dot(o1_ref[...], wo_ref[half:, :])
    )
    a_ref[...] = a
    xhat, _ = ln_parts(a)
    h = x_ref[...].astype(F32) + (xhat * norm_ref[2:3, :] + norm_ref[3:4, :])
    h_ref[...] = h
    hhat, _ = ln_parts(h)
    c_ref[...] = regroup_lanes(hhat * norm_ref[4:5, :] + norm_ref[5:6, :], size).astype(BF)


def project(size, mine, other, w_mine, w_other, x, norm, rows=256):
    tokens, model = x.shape
    row = lambda cols: pl.BlockSpec((rows, cols), lambda i: (i, 0))
    half = row(mine[0].shape[1])
    return call(
        functools.partial(project_body, size),
        (tokens // rows,),
        [half] * 4 + [whole(w_mine), whole(w_other), row(model), whole(norm)],
        [row(model)] * 3,
        [shape(tokens, model, F32), shape(tokens, model, F32), shape(tokens, model, BF)],
        (*mine, *other, w_mine, w_other, x, norm),
    )


def turn_body(m_ref, r_ref, h_ref, y_ref, norm_ref, out_ref, dm_ref, sums_ref):
    xhat, inv = ln_parts(m_ref[...] + r_ref[...].astype(F32))
    gain = norm_ref[6:7, :]
    out_ref[...] = (h_ref[...] + (xhat * gain + norm_ref[7:8, :])).astype(BF)
    z = y_ref[...].astype(F32)
    dm_ref[...] = ln_grad(xhat, inv, gain, z).astype(BF)
    add_to(sums_ref, column_sums(z, xhat))


def turn(m_part, m_other, h, y, norm, rows=256):
    tokens, model = y.shape
    row = pl.BlockSpec((rows, model), lambda i: (i, 0))
    return call(
        turn_body,
        (tokens // rows,),
        [row, row, row, row, whole(norm)],
        [row, row, pl.BlockSpec((2, model), lambda i: (0, 0))],
        [shape(tokens, model, BF), shape(tokens, model, BF), shape(2, model, F32)],
        (m_part, m_other, h, y, norm),
    )


def descend_body(
    size, dc_ref, r_ref, h_ref, a_ref, y_ref, norm_ref, dh_ref, da_ref, sums3_ref, sums2_ref
):
    dc = regroup_lanes(dc_ref[...] + r_ref[...].astype(F32), size)
    hhat, inv = ln_parts(h_ref[...])
    dh = y_ref[...].astype(F32) + ln_grad(hhat, inv, norm_ref[4:5, :], dc)
    dh_ref[...] = dh
    add_to(sums3_ref, column_sums(dc, hhat))
    ahat, inv = ln_parts(a_ref[...])
    da_ref[...] = ln_grad(ahat, inv, norm_ref[2:3, :], dh).astype(BF)
    add_to(sums2_ref, column_sums(dh, ahat))


def descend(size, dc_part, dc_other, h, a, y, norm, rows=256):
    tokens, model = y.shape
    row = pl.BlockSpec((rows, model), lambda i: (i, 0))
    sums = pl.BlockSpec((2, model), lambda i: (0, 0))
    return call(
        functools.partial(descend_body, size),
        (tokens // rows,),
        [row] * 5 + [whole(norm)],
        [row, row, sums, sums],
        [
            shape(tokens, model, F32),
            shape(tokens, model, BF),
            shape(2, model, F32),
            shape(2, model, F32),
        ],
        (dc_part, dc_other, h, a, y, norm),
    )


def up_down_body(c_ref, wu_ref, wd_ref, g_ref, s_ref, m_ref, acc):
    u = dot(c_ref[...], wu_ref[...])
    k = math.sqrt(2.0 / math.pi)
    square = u * u
    t = jnp.tanh(u * (k + (k * 0.044715) * square))
    half = 0.5 + 0.5 * t
    g = (u * half).astype(BF)
    g_ref[...] = g
    s_ref[...] = (
        half + (0.5 * u) * (1.0 - t * t) * (k + (3.0 * k * 0.044715) * square)
    ).astype(BF)
    add_to(acc, dot(g, wd_ref[...]))

    @pl.when(pl.program_id(0) == pl.num_programs(0) - 1)
    def _():
        m_ref[...] = acc[...].astype(m_ref.dtype)


def up_down(c, w_up, w_down, dtype, cols=512):
    tokens, model = c.shape
    units = 2 * model
    wide = pl.BlockSpec((tokens, cols), lambda i: (0, i))
    specs = [
        pl.BlockSpec((model, cols), lambda i: (0, i)),
        pl.BlockSpec((cols, model), lambda i: (i, 0)),
    ]
    return call(
        up_down_body,
        (units // cols,),
        [whole(c)] + specs,
        [wide, wide, pl.BlockSpec((tokens, model), lambda i: (0, 0))],
        [shape(tokens, units, BF), shape(tokens, units, BF), shape(tokens, model, dtype)],
        (c, w_up, w_down),
        scratch=[pltpu.VMEM((tokens, model), F32)],
    )


def down_up_body(dm_ref, s_ref, wu_ref, wd_ref, du_ref, dc_ref, acc):
    du = (dot(dm_ref[...], wd_ref[...], NT) * s_ref[...].astype(F32)).astype(BF)
    du_ref[...] = du
    add_to(acc, dot(du, wu_ref[...], NT))

    @pl.when(pl.program_id(0) == pl.num_programs(0) - 1)
    def _():
        dc_ref[...] = acc[...].astype(dc_ref.dtype)


def down_up(dm, slope, w_up, w_down, dtype, cols=512):
    tokens, model = dm.shape
    units = 2 * model
    wide = pl.BlockSpec((tokens, cols), lambda i: (0, i))
    specs = [
        pl.BlockSpec((model, cols), lambda i: (0, i)),
        pl.BlockSpec((cols, model), lambda i: (i, 0)),
    ]
    return call(
        down_up_body,
        (units // cols,),
        [whole(dm), wide] + specs,
        [wide, pl.BlockSpec((tokens, model), lambda i: (0, 0))],
        [shape(tokens, units, BF), shape(tokens, model, dtype)],
        (dm, slope, w_up, w_down),
        scratch=[pltpu.VMEM((tokens, model), F32)],
    )


def other_body(inverse, d0_ref, d1_ref, w0_ref, w1_ref, out_ref):
    out_ref[...] = (dot(d0_ref[...], w0_ref[...], NT) + dot(d1_ref[...], w1_ref[...], NT)).astype(BF)


def own_body(
    size, inverse, d0_ref, d1_ref, w0_ref, w1_ref, r_ref, x_ref, dh_ref, norm_ref, out_ref, sums_ref
):
    z = dot(d0_ref[...], w0_ref[...], NT) + dot(d1_ref[...], w1_ref[...], NT)
    z = regroup_lanes(z + r_ref[...].astype(F32), size)
    xhat, inv = ln_parts(x_ref[...].astype(F32))
    out_ref[...] = (dh_ref[...] + ln_grad(xhat, inv, norm_ref[0:1, :], z)).astype(BF)
    add_to(sums_ref, column_sums(z, xhat))


def input_other(inverse, d, w, span):
    width, model = d[0].shape[1], w[0].shape[0]
    part = pl.BlockSpec((span, width), lambda i, p: (p[i + 2], 0))
    return call(
        other_body,
        (2,),
        [part, part, whole(w[0]), whole(w[1])],
        pl.BlockSpec((span, model), lambda i, p: (i, 0)),
        shape(2 * span, model, BF),
        (inverse, *d, *w),
        scalars=1,
    )


def input_own(size, inverse, d, w, recv, x, dh, norm, span):
    width, model = d[0].shape[1], w[0].shape[0]
    part = pl.BlockSpec((span, width), lambda i, p: (p[i], 0))
    row = pl.BlockSpec((span, model), lambda i, p: (i, 0))
    return call(
        functools.partial(own_body, size),
        (2,),
        [part, part, whole(w[0]), whole(w[1]), row, row, row, whole(norm)],
        [row, pl.BlockSpec((2, model), lambda i, p: (0, 0))],
        [shape(2 * span, model, BF), shape(2, model, F32)],
        (inverse, *d, *w, recv, x, dh, norm),
        scalars=1,
    )


def nesterov(gradient, momentum, weight, average, step_rate, token_total):
    scaled = gradient / token_total
    new_momentum = 0.5 * momentum + scaled
    new_weight = weight - step_rate * math.sqrt(token_total) * (scaled + 0.5 * new_momentum)
    new_average = 0.5 * average + 0.5 * new_weight
    return (new_momentum, new_weight, new_average)


def tie(*values):
    return lax.optimization_barrier(values)


def per_device(
    tokens,
    cotangent,
    pair_order,
    qkv_weight,
    qkv_momentum,
    qkv_average,
    out_weight,
    out_momentum,
    out_average,
    up_weight,
    up_momentum,
    up_average,
    down_weight,
    down_momentum,
    down_average,
    norm_weight,
    norm_momentum,
    norm_average,
):
    chips = lax.axis_size("chip")
    ctx_count = lax.axis_size("ctx")
    assert ctx_count == 2 and pair_order.shape[0] == 1 and chips & (chips - 1) == 0
    levels = chips.bit_length() - 1
    chip, core, side = lax.axis_index("chip"), lax.axis_index("core"), lax.axis_index("ctx")
    count, model = tokens.shape
    span = count // 2
    token_total = count * chips * 4
    half = model // 2
    part_heads = HEADS // 4
    rows = qkv_weight.shape[0]
    units = down_weight.shape[0]
    flip = [(0, 1), (1, 0)]

    everyone = ("chip", "core", "ctx")
    full_order = list(range(levels - 1, -1, -1)) + ["core", "ctx"]
    mask_of = {"ctx": 1, "core": 2, **{n: 4 << n for n in range(levels)}}

    def exchange(x, mask):
        return lax.ppermute(x, everyone, [(i, i ^ mask) for i in range(4 * chips)])

    def to_core(x):
        return exchange(x, mask_of["core"])

    def swap_begin(x):
        return lax.ppermute(x, ("core", "ctx"), [(1, 2), (2, 1)])

    def swap_end(x, moved):
        return jnp.where(core == side, x, moved)

    def bit_of(level):
        if level == "ctx":
            return side
        if level == "core":
            return core
        return (chip >> level) & 1

    def pick(x, index, dim):
        return lax.dynamic_index_in_dim(x, index, dim, keepdims=False)

    def by_bit(bit, mine, other, axis=0):
        return jnp.stack(
            [jnp.where(bit == 0, mine, other), jnp.where(bit == 0, other, mine)], axis=axis
        )

    def masks(step):
        result = [0]
        for level in step:
            result = [m for old in result for m in (old, old | mask_of[level])]
        return result

    class Gather:
        def __init__(self, value, steps):
            self.value, self.names, self.steps = value, [], list(steps)

        def send(self):
            self.moved = [exchange(self.value, m) for m in masks(self.steps[0])[1:]]

        def join(self):
            parts = [self.value] + self.moved
            for level in reversed(self.steps.pop(0)):
                dim = sum(full_order.index(n) < full_order.index(level) for n in self.names)
                self.names.insert(dim, level)
                parts = [
                    by_bit(bit_of(level), parts[n], parts[n + 1], dim)
                    for n in range(0, len(parts), 2)
                ]
            (self.value,) = parts

    def tied(gathers, attribute, *rest):
        values, rest = tie([getattr(g, attribute) for g in gathers], rest)
        for g, v in zip(gathers, values):
            setattr(g, attribute, v)
        return rest

    high = list(range(1, levels))
    chain = high[::-1]
    far_steps = [tuple(chain[n : n + 2]) for n in range(0, len(chain), 2)]
    reduce_orders = (
        [(n,) for n in [0, "ctx"] + high],
        [(n,) for n in ["ctx", 0] + high],
    )
    chain = [0, "ctx"] + high
    short_order = [tuple(chain[n : n + 2]) for n in range(0, len(chain), 2)]
    chain = ["core", "ctx", 0] + high
    small_order = [tuple(chain[n : n + 2]) for n in range(0, len(chain), 2)]

    w = qkv_weight.astype(BF).reshape(rows, 3, 2, part_heads, 2, HEAD_DIM)
    norm_low = norm_weight.astype(BF)
    qkv_moved, norm_moved = to_core(pick(w, 1 - core, 4)), to_core(norm_low)
    local = by_bit(core, pick(w, core, 4), qkv_moved).transpose(3, 0, 1, 2, 4, 5)
    local = local.reshape(2, 2 * rows, -1)
    norm_local = jnp.pad(
        by_bit(core, norm_low, norm_moved, 1).reshape(8, -1), ((0, 0), (0, local.shape[2] - 2 * rows))
    )
    w_local = out_weight.astype(BF).reshape(rows, 2, half).transpose(1, 0, 2).reshape(2 * rows, half)
    first = Gather(
        jnp.concatenate([local[0], norm_local], axis=0), far_steps + [("ctx",), (0,)]
    )
    second = Gather(
        jnp.concatenate([local[1], w_local], axis=1), far_steps + [("ctx",), (0,)]
    )

    def join_all(gathers, *rest):
        rest = tied(gathers, "moved", *rest)
        for gather in gathers:
            gather.join()
        return tied(gathers, "value", *rest)

    def send_all(gathers):
        for gather in gathers:
            gather.send()

    first.send()
    positions = jnp.arange(2 * count, dtype=jnp.int32)
    positions, w, tokens_out, order_row = join_all(
        [first], positions, up_weight, tokens, pair_order
    )
    tied([first, second], "value")
    for _ in far_steps[1:]:
        send_all([first, second])
        join_all([first, second])
    send_all([first] + [second] * (len(far_steps) == 1))
    x_moved = swap_begin(tokens_out)
    w = w.astype(BF).reshape(rows, chips, 2, 2 * units)
    up_moved = to_core(pick(w, 1 - core, 2))
    order_row = jnp.where(core == side, order_row, to_core(order_row))[0]
    mine_first = pick(order_row, core, 0) == 0
    inverse = jnp.where(
        mine_first, jnp.array([0, 3, 1, 2], jnp.int32), jnp.array([1, 2, 0, 3], jnp.int32)
    )
    steps = jnp.arange(HEAD_DIM // 2, dtype=F32)
    frequency = jnp.exp(steps * (-math.log(10000.0) / (HEAD_DIM // 2)))
    angles = positions.astype(F32)[:, None] * frequency[None, :]
    cos, sin = jnp.cos(angles), jnp.sin(angles)
    cos_table = jnp.concatenate([cos] * 4, axis=1)
    sin_table = jnp.concatenate([-sin, sin] * 2, axis=1)
    local = by_bit(core, pick(w, core, 2).reshape(rows, 2, -1), up_moved.reshape(rows, 2, -1))
    wide = Gather(local.reshape(2 * rows, -1), far_steps)
    down_low = down_weight.astype(BF)
    cos_table, sin_table, inverse, down_low, wide.value, x_moved = join_all(
        [first] + [second] * (len(far_steps) == 1),
        cos_table,
        sin_table,
        inverse,
        down_low,
        wide.value,
        x_moved,
    )
    send_all([first, second, wide])
    w_down = lax.all_gather(down_low, ("chip", "ctx"), axis=0, tiled=True)
    x = swap_end(tokens, x_moved)
    x_other = to_core(x)
    for _ in far_steps[1:]:
        join_all([wide])
        wide.send()
    (x_other,) = join_all([first, second, wide], x_other)

    cut = wide.value.shape[-1] // 2
    ups = []
    for n in range(2):
        gather = Gather(wide.value[..., n * cut : (n + 1) * cut], [("ctx",), (0,)][:: 1 - 2 * n])
        gather.names = list(wide.names)
        ups.append(gather)
    x_other, y_out = tied([second] + ups, "value", x_other, cotangent)
    send_all([second] + ups)

    a, q0, k0, v0 = first_qkv(
        rows,
        inverse,
        x,
        x_other,
        first.value.reshape(2 * chips, 2 * rows + 8, -1),
        cos_table,
        sin_table,
        span,
    )
    gathered = first.value.reshape(2 * chips, 2 * rows + 8, -1)
    w_first = gathered[:, : 2 * rows].reshape(model, -1)
    norm = gathered[:, 2 * rows :, : 2 * rows].reshape(chips, 2, 8, 2, rows)
    norm = norm.transpose(2, 0, 3, 1, 4).reshape(8, model).astype(F32)
    q0, y_out = tie(q0, y_out)
    y_moved = swap_begin(y_out)
    own0, sent0, lse0 = attend_forward(inverse, q0, k0, v0, span)
    own0, sent0, a = join_all([second] + ups, own0, sent0, a)
    send_all(ups)
    while second.steps:
        second.send()
        own0, sent0, a = join_all([second], own0, sent0, a)
    w_rest = second.value.reshape(chips * 2, 2 * rows, -1)
    w_second = w_rest[..., :-half].reshape(model, -1)
    w_out = (
        w_rest[..., -half:]
        .reshape(chips * 2, 2, rows, half)
        .transpose(0, 2, 1, 3)
        .reshape(half, model)
    )
    w_qkv = (w_first, w_second)
    w_out_other = to_core(w_out)
    recv0 = to_core(sent0)
    q1, k1, v1 = next_qkv(a, w_second, cos_table, sin_table, span)
    own1, sent1, lse1 = attend_forward(inverse, q1, k1, v1, span)
    own1, sent1, y_moved = join_all(ups, own1, sent1, y_moved)
    w_up = jnp.concatenate([gather.value for gather in ups], axis=-1).reshape(model, -1)
    y = swap_end(cotangent, y_moved)
    recv1 = to_core(sent1)
    projected, hidden, c = project(
        rows, (own0, own1), (recv0, recv1), w_out, w_out_other, x, norm
    )
    c_other = to_core(c)
    g_other, slope_other, m_sent = up_down(c_other, w_up, w_down, BF)
    m_recv = to_core(m_sent)
    g_mine, slope_mine, m_part = up_down(c, w_up, w_down, F32)
    output, dm, sums4 = turn(m_part, m_recv, hidden, y, norm)
    output_moved = swap_begin(output)

    class Reduction:
        def __init__(self, value, names, order, wire):
            self.value, self.names, self.order, self.wire = value, names, list(order), wire
            self.flying = False

        def split(self):
            parts = [self.value]
            names = list(self.names)
            for level in self.order[0]:
                dim, bit = names.index(level), bit_of(level)
                names.pop(dim)
                parts = [pick(p, b, dim) for p in parts for b in (bit, 1 - bit)]
            self.names = names
            self.kept, self.moved = parts[0], parts[1:]

        def send(self):
            step = self.order.pop(0)
            self.moved = [exchange(p, m) for p, m in zip(self.moved, masks(step)[1:])]
            self.flying = True

        def add(self):
            v = sum([p.astype(F32) for p in self.moved], self.kept.astype(F32))
            self.value = v.astype(self.wire) if self.order else v
            self.flying = False

    def collect(flying, main):
        flying = [r for r in flying if r.flying]
        moved, main = tie([r.moved for r in flying], main)
        for r, m in zip(flying, moved):
            r.moved = m
            r.add()
        return main

    def launch(started, main):
        started = [r for r in started if r.order and not r.flying]
        for r in started:
            r.split()
        moved, main = tie([r.moved for r in started], main)
        for r, m in zip(started, moved):
            r.moved = m
            r.send()
        return main

    def slot(flying, started, main):
        return launch(flying + started, collect(flying, main))

    row_names = [n for n in full_order if n != "core"]

    def by_rows(g):
        return g.reshape((2,) * (levels + 1) + (-1, g.shape[1]))

    def halves(g):
        cut = g.shape[1] // 2
        g = by_rows(g)
        return [
            Reduction(g[..., n * cut : (n + 1) * cut], row_names, reduce_orders[n], BF)
            for n in range(2)
        ]

    def joined(pair):
        return jnp.concatenate([r.value for r in pair], axis=-1)

    dm_other = to_core(dm)
    du_mine, dc_part = down_up(dm, slope_mine, w_up, w_down, F32)
    du_other, dc_sent = down_up(dm_other, slope_other, w_up, w_down, BF)
    du_other, dc_sent, dc_part, output_moved = tie(du_other, dc_sent, dc_part, output_moved)
    output = swap_end(output, output_moved)
    dc_recv = to_core(dc_sent)
    g_two = jnp.concatenate([g_mine, g_other], axis=0)
    dm_two = jnp.concatenate([dm, dm_other], axis=0)
    down_grad = dot(g_two, dm_two, TN).astype(BF)
    down = halves(down_grad)
    du_mine, du_other = launch(down, (du_mine, du_other))
    c_two = jnp.concatenate([c, c_other], axis=0)
    du_two = jnp.concatenate([du_mine, du_other], axis=0)
    up_grad, dc_part = tie(dot(c_two, du_two, TN).astype(BF), dc_part)
    up = halves(up_grad)
    dh, da, sums3, sums2 = descend(rows, dc_part, dc_recv, hidden, projected, y, norm)
    da = slot(down, up, da)
    da_other = to_core(da)
    do = mix_gradient(inverse, da, da_other, w_out, span)
    da_two = jnp.concatenate([da, da_other], axis=0)
    o_two = jnp.concatenate(
        [jnp.concatenate([own0, own1], axis=1), jnp.concatenate([sent0, sent1], axis=1)], axis=0
    )
    out_grad, do = tie(dot(o_two, da_two, TN).astype(BF), do)
    out = [Reduction(by_rows(out_grad), row_names, reduce_orders[1], BF)]

    def attention_gradient(pair, do):
        q, k, v, own, sent, lse = (
            (q0, k0, v0, own0, sent0, lse0) if pair < 2 else (q1, k1, v1, own1, sent1, lse1)
        )
        return attend_backward(
            inverse, q, k, v, own, sent, do, lse, cos_table, sin_table, span, pair % 2, pair
        )

    def weave(first, second):
        return jnp.concatenate([t for pair in zip(first, second) for t in pair], axis=1)

    d0 = attention_gradient(0, do)
    do, d0 = slot(down, [], (do, d0))
    d1 = attention_gradient(1, do)
    do, d1 = slot(down + up, out, (do, d1))
    d_first = weave(d0, d1)
    qkv_first = [
        Reduction(by_rows(dot(a, d_first, TN).astype(BF)), row_names, reduce_orders[0], BF)
    ]
    do = launch(qkv_first, do)
    d2 = attention_gradient(2, do)
    do, d2 = slot(down + up, [], (do, d2))
    d3 = attention_gradient(3, do)
    d_second = weave(d2, d3)
    qkv_second = [Reduction(by_rows(dot(a, d_second, TN).astype(BF)), row_names, short_order, BF)]
    d_second = launch(qkv_second, d_second)
    d = (d_first, d_second)
    dx_sent = slot(down + up + out + qkv_first, [], input_other(inverse, d, w_qkv, span))
    dx_recv = to_core(dx_sent)
    dx_recv = slot(down + up + out + qkv_first, [], dx_recv)
    input_grad, sums1 = input_own(rows, inverse, d, w_qkv, dx_recv, x, dh, norm, span)
    norm_grad = jnp.concatenate([sums1, sums2, sums3, sums4], axis=0)
    share = norm_grad.reshape((8,) + (2,) * (levels + 2) + (rows,))
    share = Reduction(
        jnp.moveaxis(share, 0, levels + 2), full_order, small_order, F32
    )
    everything = down + up + out + qkv_first + qkv_second + [share]
    input_moved = swap_begin(input_grad)
    sums1 = slot(everything[:-1], [share], sums1)
    while any(r.flying for r in everything):
        sums1 = slot(everything, [], sums1)
        sums1, input_moved = tie(sums1, input_moved)
    input_grad = swap_end(input_grad, input_moved)

    def from_cores(part):
        return by_bit(core, pick(part, core, 0), to_core(pick(part, 1 - core, 0)))

    down_sum = joined(down).reshape(units, model)
    out_sum = out[0].value.reshape(rows, model)
    up_part = joined(up).reshape(2, rows, chips, 2 * units)
    up_sum = from_cores(up_part).transpose(1, 2, 0, 3).reshape(rows, -1)
    qkv_part = jnp.stack(
        [p[0].value.reshape(2, rows, 3, part_heads, HEAD_DIM) for p in (qkv_first, qkv_second)],
        axis=3,
    )
    qkv_sum = from_cores(qkv_part).transpose(1, 2, 3, 4, 0, 5).reshape(rows, -1)
    qkv_new = nesterov(qkv_sum, qkv_momentum, qkv_weight, qkv_average, rate_qkv, token_total)
    out_new = nesterov(out_sum, out_momentum, out_weight, out_average, rate_out, token_total)
    up_new = nesterov(up_sum, up_momentum, up_weight, up_average, rate_up, token_total)
    down_new = nesterov(down_sum, down_momentum, down_weight, down_average, rate_down, token_total)
    norm_new = nesterov(share.value, norm_momentum, norm_weight, norm_average, rate_norm, token_total)
    return (output, input_grad, *qkv_new, *out_new, *up_new, *down_new, *norm_new)


def solution(mesh):
    dp, ctx = mesh.shape["dp"], mesh.shape["ctx"]
    inner = Mesh(mesh.devices.reshape(dp // 2, 2, ctx), ("chip", "core", "ctx"))
    rows = P(("chip", "core", "ctx"), None)
    cols = P(None, ("chip", "core", "ctx"))
    return jax.shard_map(
        per_device,
        mesh=inner,
        in_specs=(rows, rows, P(("chip", "core"), None)) + (rows,) * 12 + (cols,) * 3,
        out_specs=(rows,) * 14 + (cols,) * 3,
        check_vma=False,
    )
```

```python
import functools
import math

import jax
import jax.numpy as jnp
from jax import lax
from jax.experimental import pallas as pl
from jax.experimental.pallas import tpu as pltpu
from jax.sharding import Mesh, PartitionSpec as P

HEADS = 16
HEAD_DIM = 64
BF = jnp.bfloat16
F32 = jnp.float32
EPS = 1e-05
VMEM_LIMIT = 56 << 20

rate_qkv = 0.04
rate_out = 0.03
rate_up = 0.03
rate_down = 0.02
rate_norm = 0.3

LOG2E = math.log2(math.e)
SCALE = 1.0 / math.sqrt(HEAD_DIM)
NT = (((1,), (1,)), ((), ()))
TN = (((0,), (0,)), ((), ()))


def dot(x, y, dims=None):
    if dims is None:
        return jnp.dot(x, y, preferred_element_type=F32)
    return lax.dot_general(x, y, dims, preferred_element_type=F32)


def call(body, grid, ins, outs, out_shape, args, scratch=(), scalars=0):
    return pl.pallas_call(
        body,
        grid_spec=pltpu.PrefetchScalarGridSpec(
            num_scalar_prefetch=scalars,
            grid=grid,
            in_specs=ins,
            out_specs=outs,
            scratch_shapes=scratch,
        ),
        out_shape=out_shape,
        compiler_params=pltpu.CompilerParams(
            dimension_semantics=("arbitrary",) * len(grid), vmem_limit_bytes=VMEM_LIMIT
        ),
    )(*args)


def shape(rows, cols, dtype):
    return jax.ShapeDtypeStruct((rows, cols), dtype)


def whole(x):
    zeros = (0,) * x.ndim
    return pl.BlockSpec(x.shape, lambda *_: zeros)


def ln_parts(v):
    centre = v - jnp.mean(v, axis=-1, keepdims=True)
    inv = lax.rsqrt(jnp.mean(centre * centre, axis=-1, keepdims=True) + EPS)
    return centre * inv, inv


def ln_grad(xhat, inv, gain, z):
    e = z * gain
    return (
        e - jnp.mean(e, axis=-1, keepdims=True) - xhat * jnp.mean(e * xhat, axis=-1, keepdims=True)
    ) * inv


def column_sums(z, xhat):
    return jnp.concatenate(
        [jnp.sum(z * xhat, axis=0, keepdims=True), jnp.sum(z, axis=0, keepdims=True)], axis=0
    )


def add_to(ref, value):
    @pl.when(pl.program_id(0) == 0)
    def _():
        ref[...] = value

    @pl.when(pl.program_id(0) > 0)
    def _():
        ref[...] += value


def regroup_lanes(u, size):
    lane = lax.broadcasted_iota(jnp.int32, (u.shape[0], 128), 1) % (4 * size)
    groups = []
    for start in range(0, u.shape[1], 128):
        w = u[:, start : start + 128]
        w = jnp.where(
            (lane >= size) & (lane < 2 * size),
            pltpu.roll(w, 128 - size, 1),
            jnp.where((lane >= 2 * size) & (lane < 3 * size), pltpu.roll(w, size, 1), w),
        )
        groups.append(w)
    return jnp.concatenate(groups, axis=1)


def swapped_halves(u):
    lane = lax.broadcasted_iota(jnp.int32, u.shape, 1) % HEAD_DIM
    return jnp.where(lane < HEAD_DIM // 2, pltpu.roll(u, 96, 1), pltpu.roll(u, 32, 1))


def qkv_rows(a, w, cos, sin, q_ref, k_ref, v_ref):
    width = q_ref.shape[1]
    for part, ref in enumerate((q_ref, k_ref)):
        rows = dot(a, w[:, part * width : (part + 1) * width])
        for group in range(width // 128):
            u = rows[:, group * 128 : (group + 1) * 128]
            ref[:, group * 128 : (group + 1) * 128] = (u * cos + swapped_halves(u) * sin).astype(BF)
    v_ref[...] = dot(a, w[:, 2 * width :]).astype(BF)


def first_qkv_body(
    size,
    inverse,
    own_ref,
    other_ref,
    w_ref,
    cos_ref,
    sin_ref,
    a_ref,
    q_ref,
    k_ref,
    v_ref,
):
    owners = w_ref.shape[0]
    x = jnp.where(pl.program_id(0) < 2, own_ref[...], other_ref[...])
    xhat, _ = ln_parts(x.astype(F32))
    norm = jnp.concatenate(
        [
            w_ref[n + side, 2 * size : 2 * size + 8, core * size : (core + 1) * size]
            for n in range(0, owners, 2)
            for core in range(2)
            for side in range(2)
        ],
        axis=1,
    ).astype(F32)
    a = (xhat * norm[0:1, :] + norm[1:2, :]).astype(BF)
    a_ref[...] = a
    w = w_ref[:, : 2 * size, :].reshape(2 * size * owners, w_ref.shape[2])
    qkv_rows(regroup_lanes(a, size), w, cos_ref[...], sin_ref[...], q_ref, k_ref, v_ref)


def next_qkv_body(a_ref, w_ref, cos_ref, sin_ref, q_ref, k_ref, v_ref):
    qkv_rows(a_ref[...], w_ref[...], cos_ref[...], sin_ref[...], q_ref, k_ref, v_ref)


def first_qkv(size, inverse, own, other, w_qkv, cos, sin, span):
    tokens, model = 2 * own.shape[0], own.shape[1]
    width = w_qkv.shape[2] // 3
    row = lambda cols: pl.BlockSpec((span, cols), lambda i, p: (p[i], 0))
    return call(
        functools.partial(first_qkv_body, size),
        (tokens // span,),
        [
            pl.BlockSpec((span, model), lambda i, p: (jnp.minimum(i, 1), 0)),
            pl.BlockSpec((span, model), lambda i, p: (jnp.maximum(i - 2, 0), 0)),
            whole(w_qkv),
            row(128),
            row(128),
        ],
        [row(model), row(width), row(width), row(width)],
        [shape(tokens, model, BF)] + [shape(tokens, width, BF)] * 3,
        (inverse, own, other, w_qkv, cos, sin),
        scalars=1,
    )


def next_qkv(a, w_qkv, cos, sin, span):
    tokens, model = a.shape
    width = w_qkv.shape[1] // 3
    row = lambda cols: pl.BlockSpec((span, cols), lambda i: (i, 0))
    return call(
        next_qkv_body,
        (tokens // span,),
        [row(model), whole(w_qkv), row(128), row(128)],
        [row(width)] * 3,
        [shape(tokens, width, BF)] * 3,
        (a, w_qkv, cos, sin),
    )


def head_mask(shape_):
    return lax.broadcasted_iota(jnp.int32, shape_, 1) < HEAD_DIM


def forward_body(place, q_ref, k_ref, v_ref, own_ref, sent_ref, lse_ref):
    span = own_ref.shape[0] // 2
    first = head_mask((span, 128))
    causal = lax.broadcasted_iota(jnp.int32, (span, span), 0) <= lax.broadcasted_iota(
        jnp.int32, (span, span), 1
    )
    turned = v_ref[...].T
    for block in range(k_ref.shape[0] // span):
        rows = slice(block * span, (block + 1) * span)
        q = q_ref[rows, :]
        zero = jnp.zeros_like(q)
        heads = []
        for head in range(2):
            mine = jnp.where(first, q, zero) if head == 0 else jnp.where(first, zero, q)
            s = dot(k_ref[: rows.stop, :], mine, NT) * (SCALE * LOG2E)
            diagonal = jnp.where(causal, s[rows.start :], -jnp.inf)
            s = jnp.concatenate([s[: rows.start], diagonal], axis=0) if block else diagonal
            top = jnp.max(s, axis=0, keepdims=True)
            p = jnp.exp2(s - top)
            total = jnp.sum(p, axis=0, keepdims=True)
            lanes = slice(head * HEAD_DIM, (head + 1) * HEAD_DIM)
            heads.append(dot(turned[lanes, : rows.stop], p.astype(BF)) / total)
            lse_ref[head * 8 : head * 8 + 1, rows] = top + jnp.log2(total)
        o = jnp.concatenate(heads, axis=0).T.astype(BF)
        at = place[block]

        @pl.when(at < 2)
        def _():
            own_ref[pl.ds(pl.multiple_of(at * span, span), span), :] = o

        @pl.when(at >= 2)
        def _():
            sent_ref[pl.ds(pl.multiple_of((at - 2) * span, span), span), :] = o


def attend_forward(place, q, k, v):
    tokens, width = q.shape
    pairs = width // 128
    full = pl.BlockSpec((tokens, 128), lambda h, p: (0, h))
    half = pl.BlockSpec((tokens // 2, 128), lambda h, p: (0, h))
    return call(
        forward_body,
        (pairs,),
        [full, full, full],
        [half, half, pl.BlockSpec((16, tokens), lambda h, p: (h, 0))],
        [
            shape(tokens // 2, width, BF),
            shape(tokens // 2, width, BF),
            shape(16 * pairs, tokens, F32),
        ],
        (place, q, k, v),
        scalars=1,
    )


def backward_body(
    place,
    q_ref,
    k_ref,
    v_ref,
    own_ref,
    sent_ref,
    g_ref,
    lse_ref,
    cos_ref,
    sin_ref,
    dq_ref,
    dk_ref,
    dv_ref,
    dk_acc,
    dv_acc,
):
    span = own_ref.shape[0] // 2
    rows = span // 2
    first = head_mask((rows, 128))
    zero = jnp.zeros((rows, 128), BF)
    causal = lax.broadcasted_iota(jnp.int32, (rows, rows), 0) <= lax.broadcasted_iota(
        jnp.int32, (rows, rows), 1
    )
    turned = k_ref[...].T
    dk_acc[...] = jnp.zeros_like(dk_acc)
    dv_acc[...] = jnp.zeros_like(dv_acc)
    for block in range(q_ref.shape[0] // rows):
        here = slice(block * rows, (block + 1) * rows)
        q, g = q_ref[here, :], g_ref[here, :]
        at = place[block * rows // span]
        start = pl.multiple_of((at % 2) * span + block * rows % span, rows)
        o = jnp.where(at < 2, own_ref[pl.ds(start, rows), :], sent_ref[pl.ds(start, rows), :])
        prod = (o.astype(F32) * g.astype(F32)).T
        parts = []
        for head in range(2):
            lanes = slice(head * HEAD_DIM, (head + 1) * HEAD_DIM)
            q_mine = jnp.where(first, q, zero) if head == 0 else jnp.where(first, zero, q)
            g_mine = jnp.where(first, g, zero) if head == 0 else jnp.where(first, zero, g)
            inner = jnp.sum(prod[lanes], axis=0, keepdims=True)
            s = dot(k_ref[: here.stop, :], q_mine, NT)
            p = jnp.exp2(s * (SCALE * LOG2E) - lse_ref[head * 8 : head * 8 + 1, here])
            diagonal = jnp.where(causal, p[here.start :], 0.0)
            p = jnp.concatenate([p[: here.start], diagonal], axis=0) if block else diagonal
            dp = dot(v_ref[: here.stop, :], g_mine, NT)
            ds = (p * (dp - inner)).astype(BF)
            dv_acc[: here.stop, :] += dot(p.astype(BF), g_mine)
            dk_acc[: here.stop, :] += dot(ds, q_mine)
            parts.append(dot(turned[lanes, : here.stop], ds))
        dq = jnp.concatenate(parts, axis=0).T * SCALE
        dq_ref[here, :] = (dq * cos_ref[here, :] - swapped_halves(dq) * sin_ref[here, :]).astype(BF)
    dk = dk_acc[...] * SCALE
    dk_ref[...] = (dk * cos_ref[...] - swapped_halves(dk) * sin_ref[...]).astype(BF)
    dv_ref[...] = dv_acc[...].astype(BF)


def attend_backward(place, q, k, v, own, sent, g, lse, cos, sin, pair, g_pair):
    tokens = q.shape[0]
    full = pl.BlockSpec((tokens, 128), lambda i, p: (0, pair))
    side = pl.BlockSpec((tokens // 2, 128), lambda i, p: (0, pair))
    out = pl.BlockSpec((tokens, 128), lambda i, p: (0, 0))
    return call(
        backward_body,
        (1,),
        [
            full,
            full,
            full,
            side,
            side,
            pl.BlockSpec((tokens, 128), lambda i, p: (0, g_pair)),
            pl.BlockSpec((16, tokens), lambda i, p: (pair, 0)),
            out,
            out,
        ],
        [out, out, out],
        [shape(tokens, 128, BF)] * 3,
        (place, q, k, v, own, sent, g, lse, cos, sin),
        scratch=[pltpu.VMEM((tokens, 128), F32), pltpu.VMEM((tokens, 128), F32)],
        scalars=1,
    )


def mix_body(inverse, own_ref, other_ref, w_ref, out_ref):
    index = pl.program_id(0)

    @pl.when(index < 2)
    def _():
        out_ref[...] = dot(own_ref[...], w_ref[...], NT).astype(BF)

    @pl.when(index >= 2)
    def _():
        out_ref[...] = dot(other_ref[...], w_ref[...], NT).astype(BF)


def mix_gradient(inverse, own, other, w_out, span):
    model = own.shape[1]
    width = w_out.shape[0]
    return call(
        mix_body,
        (4,),
        [
            pl.BlockSpec((span, model), lambda i, p: (jnp.minimum(i, 1), 0)),
            pl.BlockSpec((span, model), lambda i, p: (jnp.maximum(i - 2, 0), 0)),
            whole(w_out),
        ],
        pl.BlockSpec((span, width), lambda i, p: (p[i], 0)),
        shape(4 * span, width, BF),
        (inverse, own, other, w_out),
        scalars=1,
    )


def project_body(
    size, m0_ref, m1_ref, o0_ref, o1_ref, wm_ref, wo_ref, x_ref, norm_ref, a_ref, h_ref, c_ref
):
    half = m0_ref.shape[1]
    a = (
        dot(m0_ref[...], wm_ref[:half, :])
        + dot(m1_ref[...], wm_ref[half:, :])
        + dot(o0_ref[...], wo_ref[:half, :])
        + dot(o1_ref[...], wo_ref[half:, :])
    )
    a_ref[...] = a
    xhat, _ = ln_parts(a)
    h = x_ref[...].astype(F32) + (xhat * norm_ref[2:3, :] + norm_ref[3:4, :])
    h_ref[...] = h
    hhat, _ = ln_parts(h)
    c_ref[...] = regroup_lanes((hhat * norm_ref[4:5, :] + norm_ref[5:6, :]).astype(BF), size)


def project(size, mine, other, w_mine, w_other, x, norm, rows=256):
    tokens, model = x.shape
    row = lambda cols: pl.BlockSpec((rows, cols), lambda i: (i, 0))
    half = row(mine[0].shape[1])
    return call(
        functools.partial(project_body, size),
        (tokens // rows,),
        [half] * 4 + [whole(w_mine), whole(w_other), row(model), whole(norm)],
        [row(model)] * 3,
        [shape(tokens, model, F32), shape(tokens, model, F32), shape(tokens, model, BF)],
        (*mine, *other, w_mine, w_other, x, norm),
    )


def turn_body(m_ref, r_ref, h_ref, y_ref, norm_ref, out_ref, dm_ref, sums_ref):
    xhat, inv = ln_parts(m_ref[...] + r_ref[...].astype(F32))
    gain = norm_ref[6:7, :]
    out_ref[...] = (h_ref[...] + (xhat * gain + norm_ref[7:8, :])).astype(BF)
    z = y_ref[...].astype(F32)
    dm_ref[...] = ln_grad(xhat, inv, gain, z).astype(BF)
    add_to(sums_ref, column_sums(z, xhat))


def turn(m_part, m_other, h, y, norm, rows=256):
    tokens, model = y.shape
    row = pl.BlockSpec((rows, model), lambda i: (i, 0))
    return call(
        turn_body,
        (tokens // rows,),
        [row, row, row, row, whole(norm)],
        [row, row, pl.BlockSpec((2, model), lambda i: (0, 0))],
        [shape(tokens, model, BF), shape(tokens, model, BF), shape(2, model, F32)],
        (m_part, m_other, h, y, norm),
    )


def descend_body(
    size, dc_ref, r_ref, h_ref, a_ref, y_ref, norm_ref, dh_ref, da_ref, sums3_ref, sums2_ref
):
    dc = regroup_lanes(dc_ref[...] + r_ref[...].astype(F32), size)
    hhat, inv = ln_parts(h_ref[...])
    dh = y_ref[...].astype(F32) + ln_grad(hhat, inv, norm_ref[4:5, :], dc)
    dh_ref[...] = dh
    add_to(sums3_ref, column_sums(dc, hhat))
    ahat, inv = ln_parts(a_ref[...])
    da_ref[...] = ln_grad(ahat, inv, norm_ref[2:3, :], dh).astype(BF)
    add_to(sums2_ref, column_sums(dh, ahat))


def descend(size, dc_part, dc_other, h, a, y, norm, rows=256):
    tokens, model = y.shape
    row = pl.BlockSpec((rows, model), lambda i: (i, 0))
    sums = pl.BlockSpec((2, model), lambda i: (0, 0))
    return call(
        functools.partial(descend_body, size),
        (tokens // rows,),
        [row] * 5 + [whole(norm)],
        [row, row, sums, sums],
        [
            shape(tokens, model, F32),
            shape(tokens, model, BF),
            shape(2, model, F32),
            shape(2, model, F32),
        ],
        (dc_part, dc_other, h, a, y, norm),
    )


def mlp_weights(w, cols):
    owners, rows, model = w.shape
    down = w.reshape(owners, 2, rows // 2, model)
    up = w.reshape(owners, 4, rows // 4, model)
    per = cols // (rows // 2)
    halves = model // cols
    return (
        [up, down],
        [
            pl.BlockSpec(
                (owners, None, rows // 4, cols), lambda i: (0, 2 + i // halves, 0, i % halves)
            ),
            pl.BlockSpec((per, None, rows // 2, model), lambda i: (i, 0, 0, 0)),
        ],
    )


def flat(ref):
    w = ref[...]
    return w.reshape(w.shape[0] * w.shape[1], w.shape[2])


def add_through(acc, out_ref, value):
    step, last = pl.program_id(0), pl.num_programs(0) - 1

    @pl.when(step == 0)
    def _():
        acc[...] = value

    @pl.when((step > 0) & (step < last))
    def _():
        acc[...] += value

    @pl.when(step == last)
    def _():
        out_ref[...] = (acc[...] + value).astype(out_ref.dtype)


def up_down_body(c_ref, wu_ref, wd_ref, g_ref, s_ref, m_ref, acc):
    u = dot(c_ref[...], flat(wu_ref))
    k = math.sqrt(2.0 / math.pi)
    square = u * u
    t = jnp.tanh(u * (k + (k * 0.044715) * square))
    half = 0.5 + 0.5 * t
    g = (u * half).astype(BF)
    g_ref[...] = g
    s_ref[...] = (
        half + (0.5 * u) * (1.0 - t * t) * (k + (3.0 * k * 0.044715) * square)
    ).astype(BF)
    add_through(acc, m_ref, dot(g, flat(wd_ref)))


def up_down(c, w_mlp, dtype, cols=512):
    tokens, model = c.shape
    units = 2 * model
    wide = pl.BlockSpec((tokens, cols), lambda i: (0, i))
    weights, specs = mlp_weights(w_mlp, cols)
    return call(
        up_down_body,
        (units // cols,),
        [whole(c)] + specs,
        [wide, wide, pl.BlockSpec((tokens, model), lambda i: (0, 0))],
        [shape(tokens, units, BF), shape(tokens, units, BF), shape(tokens, model, dtype)],
        (c, *weights),
        scratch=[pltpu.VMEM((tokens, model), F32)],
    )


def down_up_body(dm_ref, s_ref, wu_ref, wd_ref, du_ref, dc_ref, acc):
    du = (dot(dm_ref[...], flat(wd_ref), NT) * s_ref[...].astype(F32)).astype(BF)
    du_ref[...] = du
    add_through(acc, dc_ref, dot(du, flat(wu_ref), NT))


def down_up(dm, slope, w_mlp, dtype, cols=512):
    tokens, model = dm.shape
    units = 2 * model
    wide = pl.BlockSpec((tokens, cols), lambda i: (0, i))
    weights, specs = mlp_weights(w_mlp, cols)
    return call(
        down_up_body,
        (units // cols,),
        [whole(dm), wide] + specs,
        [wide, pl.BlockSpec((tokens, model), lambda i: (0, 0))],
        [shape(tokens, units, BF), shape(tokens, model, dtype)],
        (dm, slope, *weights),
        scratch=[pltpu.VMEM((tokens, model), F32)],
    )


def other_body(inverse, d0_ref, d1_ref, w0_ref, w1_ref, out_ref):
    out_ref[...] = (dot(d0_ref[...], w0_ref[...], NT) + dot(d1_ref[...], w1_ref[...], NT)).astype(BF)


def own_body(
    inverse, d0_ref, d1_ref, w0_ref, w1_ref, r_ref, x_ref, dh_ref, norm_ref, out_ref, sums_ref
):
    z = dot(d0_ref[...], w0_ref[...], NT) + dot(d1_ref[...], w1_ref[...], NT)
    z = z + r_ref[...].astype(F32)
    xhat, inv = ln_parts(x_ref[...].astype(F32))
    out_ref[...] = (dh_ref[...] + ln_grad(xhat, inv, norm_ref[0:1, :], z)).astype(BF)
    add_to(sums_ref, column_sums(z, xhat))


def input_other(inverse, d, w, span):
    width, model = d[0].shape[1], w[0].shape[0]
    part = pl.BlockSpec((span, width), lambda i, p: (p[i + 2], 0))
    return call(
        other_body,
        (2,),
        [part, part, whole(w[0]), whole(w[1])],
        pl.BlockSpec((span, model), lambda i, p: (i, 0)),
        shape(2 * span, model, BF),
        (inverse, *d, *w),
        scalars=1,
    )


def input_own(inverse, d, w, recv, x, dh, norm, span):
    width, model = d[0].shape[1], w[0].shape[0]
    part = pl.BlockSpec((span, width), lambda i, p: (p[i], 0))
    row = pl.BlockSpec((span, model), lambda i, p: (i, 0))
    return call(
        own_body,
        (2,),
        [part, part, whole(w[0]), whole(w[1]), row, row, row, whole(norm)],
        [row, pl.BlockSpec((2, model), lambda i, p: (0, 0))],
        [shape(2 * span, model, BF), shape(2, model, F32)],
        (inverse, *d, *w, recv, x, dh, norm),
        scalars=1,
    )


def nesterov(gradient, momentum, weight, average, step_rate, token_total):
    scaled = gradient / token_total
    new_momentum = 0.5 * momentum + scaled
    new_weight = weight - step_rate * math.sqrt(token_total) * (scaled + 0.5 * new_momentum)
    new_average = 0.5 * average + 0.5 * new_weight
    return (new_momentum, new_weight, new_average)


def tie(*values):
    return lax.optimization_barrier(values)


def per_device(
    tokens,
    cotangent,
    pair_order,
    qkv_weight,
    qkv_momentum,
    qkv_average,
    out_weight,
    out_momentum,
    out_average,
    up_weight,
    up_momentum,
    up_average,
    down_weight,
    down_momentum,
    down_average,
    norm_weight,
    norm_momentum,
    norm_average,
):
    chips = lax.axis_size("chip")
    ctx_count = lax.axis_size("ctx")
    assert ctx_count == 2 and pair_order.shape[0] == 1 and chips & (chips - 1) == 0
    levels = chips.bit_length() - 1
    chip, core, side = lax.axis_index("chip"), lax.axis_index("core"), lax.axis_index("ctx")
    count, model = tokens.shape
    span = count // 2
    token_total = count * chips * 4
    half = model // 2
    part_heads = HEADS // 4
    rows = qkv_weight.shape[0]
    units = down_weight.shape[0]
    flip = [(0, 1), (1, 0)]

    everyone = ("chip", "core", "ctx")
    full_order = list(range(levels - 1, -1, -1)) + ["core", "ctx"]
    mask_of = {"ctx": 1, "core": 2, **{n: 4 << n for n in range(levels)}}

    def exchange(x, mask):
        return lax.ppermute(x, everyone, [(i, i ^ mask) for i in range(4 * chips)])

    def to_core(x):
        return exchange(x, mask_of["core"])

    def swap_begin(x):
        return lax.ppermute(x, ("core", "ctx"), [(1, 2), (2, 1)])

    def swap_end(x, moved):
        return jnp.where(core == side, x, moved)

    def bit_of(level):
        if level == "ctx":
            return side
        if level == "core":
            return core
        return (chip >> level) & 1

    def pick(x, index, dim):
        return lax.dynamic_index_in_dim(x, index, dim, keepdims=False)

    def by_bit(bit, mine, other, axis=0):
        return jnp.stack(
            [jnp.where(bit == 0, mine, other), jnp.where(bit == 0, other, mine)], axis=axis
        )

    def masks(step):
        result = [0]
        for level in step:
            result = [m for old in result for m in (old, old | mask_of[level])]
        return result

    class Gather:
        def __init__(self, value, steps, names=()):
            self.value, self.names, self.steps = value, list(names), list(steps)

        def send(self):
            self.moved = [exchange(self.value, m) for m in masks(self.steps[0])[1:]]

        def join(self):
            parts = [self.value] + self.moved
            for level in reversed(self.steps.pop(0)):
                dim = sum(full_order.index(n) < full_order.index(level) for n in self.names)
                self.names.insert(dim, level)
                parts = [
                    by_bit(bit_of(level), parts[n], parts[n + 1], dim)
                    for n in range(0, len(parts), 2)
                ]
            (self.value,) = parts

    def tied(gathers, attribute, *rest):
        values, rest = tie([getattr(g, attribute) for g in gathers], rest)
        for g, v in zip(gathers, values):
            setattr(g, attribute, v)
        return rest

    high = list(range(1, levels))
    chain = high[::-1]
    far_steps = [tuple(chain[n : n + 2]) for n in range(0, len(chain), 2)]
    reduce_orders = (
        [(n,) for n in [0, "ctx"] + high],
        [(n,) for n in ["ctx", 0] + high],
    )
    chain = [0, "ctx"] + high
    short_order = [tuple(chain[n : n + 2]) for n in range(0, len(chain), 2)]
    chain = ["core", "ctx", 0] + high
    small_order = [tuple(chain[n : n + 2]) for n in range(0, len(chain), 2)]

    w = qkv_weight.astype(BF).reshape(rows, 3, 2, part_heads, 2, HEAD_DIM)
    norm_low = norm_weight.astype(BF)
    qkv_moved, norm_moved = to_core(pick(w, 1 - core, 4)), to_core(norm_low)
    local = by_bit(core, pick(w, core, 4), qkv_moved).transpose(3, 0, 1, 2, 4, 5)
    local = local.reshape(2, 2 * rows, -1)
    norm_local = jnp.pad(
        by_bit(core, norm_low, norm_moved, 1).reshape(8, -1), ((0, 0), (0, local.shape[2] - 2 * rows))
    )
    w_local = out_weight.astype(BF).reshape(rows, 2, half).transpose(1, 0, 2)
    first = Gather(
        jnp.concatenate([local[0], norm_local], axis=0), far_steps + [("ctx",), (0,)]
    )
    second = Gather(
        jnp.concatenate([local[1].reshape(2, rows, -1), w_local], axis=2),
        far_steps + [("ctx",), (0,)],
        ["core"],
    )

    def join_all(gathers, *rest):
        rest = tied(gathers, "moved", *rest)
        for gather in gathers:
            gather.join()
        return tied(gathers, "value", *rest)

    def send_all(gathers):
        for gather in gathers:
            gather.send()

    x_moved = swap_begin(tokens)
    first.send()
    positions, order_row, up_low, x_moved = join_all(
        [first], jnp.arange(2 * count, dtype=jnp.int32), pair_order, up_weight, x_moved
    )
    x = swap_end(tokens, x_moved)
    tied([first, second], "value")
    for _ in far_steps[1:]:
        send_all([first, second])
        join_all([first, second])
    send_all([first] + [second] * (len(far_steps) == 1))
    order_row = jnp.where(core == side, order_row, to_core(order_row))[0]
    mine_first = pick(order_row, core, 0) == 0
    inverse = jnp.where(
        mine_first, jnp.array([0, 3, 1, 2], jnp.int32), jnp.array([1, 2, 0, 3], jnp.int32)
    )
    place = jnp.where(
        mine_first, jnp.array([0, 2, 3, 1], jnp.int32), jnp.array([2, 0, 1, 3], jnp.int32)
    )
    steps = jnp.arange(HEAD_DIM // 2, dtype=F32)
    frequency = jnp.exp(steps * (-math.log(10000.0) / (HEAD_DIM // 2)))
    angles = positions.astype(F32)[:, None] * frequency[None, :]
    cos, sin = jnp.cos(angles), jnp.sin(angles)
    cos_table = jnp.concatenate([cos] * 4, axis=1)
    sin_table = jnp.concatenate([-sin, sin] * 2, axis=1)
    x_other = to_core(x)
    w = up_low.astype(BF).reshape(rows, chips, 2, 2 * units)
    up_moved = to_core(pick(w, 1 - core, 2))
    local = by_bit(core, pick(w, core, 2).reshape(rows, 2, -1), up_moved.reshape(rows, 2, -1))
    local = local.transpose(2, 0, 1, 3)
    wide = local.shape[-1]
    per_owner = jnp.concatenate(
        [down_weight.astype(BF).reshape(-1, wide), local.reshape(-1, wide)], axis=0
    )
    w_mlp = lax.all_gather(per_owner, ("chip", "ctx"), axis=0)
    inverse, place, x_other = join_all(
        [first] + [second] * (len(far_steps) == 1), inverse, place, x_other
    )
    send_all([first, second])
    x_other, cos_table, sin_table, y_out = join_all(
        [first, second], x_other, cos_table, sin_table, cotangent
    )
    second.send()

    a, q0, k0, v0 = first_qkv(
        rows,
        inverse,
        x,
        x_other,
        first.value.reshape(2 * chips, 2 * rows + 8, -1),
        cos_table,
        sin_table,
        span,
    )
    gathered = first.value.reshape(2 * chips, 2 * rows + 8, -1)
    w_first = gathered[:, : 2 * rows].reshape(chips, 2, 2, rows, -1)
    w_first = w_first.transpose(0, 2, 1, 3, 4).reshape(model, -1)
    norm = gathered[:, 2 * rows :, : 2 * rows].reshape(chips, 2, 8, 2, rows)
    norm = norm.transpose(2, 0, 3, 1, 4).reshape(8, model).astype(F32)
    q0, y_out = tie(q0, y_out)
    y_moved = swap_begin(y_out)
    own0, sent0, lse0 = attend_forward(place, q0, k0, v0)
    own0, sent0, a = join_all([second], own0, sent0, a)
    while second.steps:
        second.send()
        own0, sent0, a = join_all([second], own0, sent0, a)
    w_rest = second.value.reshape(chips, 2, 2, rows, -1)
    w_second = w_rest[..., :-half].reshape(model, -1)
    w_out = w_rest[..., -half:].transpose(0, 2, 3, 1, 4).reshape(half, model)
    w_qkv = (w_first, w_second)
    w_out_other = to_core(w_out)
    recv0 = to_core(sent0)
    q1, k1, v1 = next_qkv(a, w_second, cos_table, sin_table, span)
    own1, sent1, lse1 = attend_forward(place, q1, k1, v1)
    own1, sent1, y_moved = tie(own1, sent1, y_moved)
    y = swap_end(cotangent, y_moved)
    recv1 = to_core(sent1)
    projected, hidden, c = project(
        rows, (own0, own1), (recv0, recv1), w_out, w_out_other, x, norm
    )
    c_other = to_core(c)
    g_other, slope_other, m_sent = up_down(c_other, w_mlp, BF)
    m_recv = to_core(m_sent)
    g_mine, slope_mine, m_part = up_down(c, w_mlp, F32)
    output, dm, sums4 = turn(m_part, m_recv, hidden, y, norm)
    output_moved = swap_begin(output)

    class Reduction:
        def __init__(self, value, names, order, wire):
            self.value, self.names, self.order, self.wire = value, names, list(order), wire
            self.flying = False

        def split(self):
            parts = [self.value]
            names = list(self.names)
            for level in self.order[0]:
                dim, bit = names.index(level), bit_of(level)
                names.pop(dim)
                parts = [pick(p, b, dim) for p in parts for b in (bit, 1 - bit)]
            self.names = names
            self.kept, self.moved = parts[0], parts[1:]

        def send(self):
            step = self.order.pop(0)
            self.moved = [exchange(p, m) for p, m in zip(self.moved, masks(step)[1:])]
            self.flying = True

        def add(self):
            v = sum([p.astype(F32) for p in self.moved], self.kept.astype(F32))
            self.value = v.astype(self.wire) if self.order else v
            self.flying = False

    def collect(flying, main):
        flying = [r for r in flying if r.flying]
        moved, main = tie([r.moved for r in flying], main)
        for r, m in zip(flying, moved):
            r.moved = m
            r.add()
        return main

    def launch(started, main):
        started = [r for r in started if r.order and not r.flying]
        for r in started:
            r.split()
        moved, main = tie([r.moved for r in started], main)
        for r, m in zip(started, moved):
            r.moved = m
            r.send()
        return main

    def slot(flying, started, main):
        return launch(flying + started, collect(flying, main))

    def by_rows(g, order, owned):
        names = [n for n in full_order if n != "core" or owned is False]
        return Reduction(g.reshape((2,) * len(names) + (-1, g.shape[1])), names, order, BF)

    def halves(g, owned):
        cut = g.shape[1] // 2
        return [
            by_rows(g[:, n * cut : (n + 1) * cut], reduce_orders[n], owned) for n in range(2)
        ]

    def joined(pair):
        return jnp.concatenate([r.value for r in pair], axis=-1)

    dm_other = to_core(dm)
    du_mine, dc_part = down_up(dm, slope_mine, w_mlp, F32)
    du_other, dc_sent = down_up(dm_other, slope_other, w_mlp, BF)
    du_other, dc_sent, dc_part, output_moved = tie(du_other, dc_sent, dc_part, output_moved)
    output = swap_end(output, output_moved)
    dc_recv = to_core(dc_sent)
    g_two = jnp.concatenate([g_mine, g_other], axis=0)
    dm_two = jnp.concatenate([dm, dm_other], axis=0)
    down_grad = dot(g_two, dm_two, TN).astype(BF)
    down = halves(down_grad, True)
    du_mine, du_other = launch(down, (du_mine, du_other))
    c_two = jnp.concatenate([c, c_other], axis=0)
    du_two = jnp.concatenate([du_mine, du_other], axis=0)
    up_grad, dc_part = tie(dot(c_two, du_two, TN).astype(BF), dc_part)
    up = halves(up_grad, None)
    dh, da, sums3, sums2 = descend(rows, dc_part, dc_recv, hidden, projected, y, norm)
    da = slot(down, up, da)
    da_other = to_core(da)
    do = mix_gradient(inverse, da, da_other, w_out, span)
    da_two = jnp.concatenate([da, da_other], axis=0)
    o_two = jnp.concatenate(
        [jnp.concatenate([own0, own1], axis=1), jnp.concatenate([sent0, sent1], axis=1)], axis=0
    )
    out_grad, do = tie(dot(o_two, da_two, TN).astype(BF), do)
    out = [by_rows(out_grad, short_order, True)]

    def attention_gradient(pair, do):
        q, k, v, own, sent, lse = (
            (q0, k0, v0, own0, sent0, lse0) if pair < 2 else (q1, k1, v1, own1, sent1, lse1)
        )
        return attend_backward(
            place, q, k, v, own, sent, do, lse, cos_table, sin_table, pair % 2, pair
        )

    def weave(first, second):
        return jnp.concatenate([t for pair in zip(first, second) for t in pair], axis=1)

    d0 = attention_gradient(0, do)
    do, d0 = slot(down, [], (do, d0))
    d1 = attention_gradient(1, do)
    do, d1 = slot(down + up, out, (do, d1))
    d_first = weave(d0, d1)
    qkv_first = [by_rows(dot(a, d_first, TN).astype(BF), short_order, False)]
    do = launch(qkv_first, do)
    d2 = attention_gradient(2, do)
    do, d2 = slot(down + up + out, [], (do, d2))
    d3 = attention_gradient(3, do)
    d_second = weave(d2, d3)
    qkv_second = [by_rows(dot(a, d_second, TN).astype(BF), short_order, False)]
    d_second = launch(qkv_second, d_second)
    d_second = slot(down + up + out + qkv_first, [], d_second)
    d = (d_first, d_second)
    dx_recv = to_core(input_other(inverse, d, w_qkv, span))
    input_grad, sums1 = input_own(inverse, d, w_qkv, dx_recv, x, dh, norm, span)
    input_moved = swap_begin(input_grad)
    norm_grad = jnp.concatenate([sums1, sums2, sums3, sums4], axis=0)
    share = norm_grad.reshape((8,) + (2,) * (levels + 2) + (rows,))
    share = Reduction(jnp.moveaxis(share, 0, levels + 2), full_order, small_order, F32)
    everything = down + up + out + qkv_first + qkv_second + [share]
    sums1 = slot(qkv_second, [share], sums1)
    sums1, input_moved = tie(sums1, input_moved)
    while any(r.flying for r in everything):
        sums1 = slot(everything, [], sums1)
    input_grad = swap_end(input_grad, input_moved)

    def from_cores(part):
        return by_bit(core, pick(part, core, 0), to_core(pick(part, 1 - core, 0)))

    down_sum = joined(down).reshape(units, model)
    out_sum = out[0].value.reshape(rows, model)
    up_part = joined(up).reshape(2, rows, chips, 2 * units)
    up_sum = from_cores(up_part).transpose(1, 2, 0, 3).reshape(rows, -1)
    qkv_part = jnp.stack(
        [p[0].value.reshape(2, rows, 3, part_heads, HEAD_DIM) for p in (qkv_first, qkv_second)],
        axis=3,
    )
    qkv_sum = from_cores(qkv_part).transpose(1, 2, 3, 4, 0, 5).reshape(rows, -1)
    qkv_new = nesterov(qkv_sum, qkv_momentum, qkv_weight, qkv_average, rate_qkv, token_total)
    out_new = nesterov(out_sum, out_momentum, out_weight, out_average, rate_out, token_total)
    up_new = nesterov(up_sum, up_momentum, up_weight, up_average, rate_up, token_total)
    down_new = nesterov(down_sum, down_momentum, down_weight, down_average, rate_down, token_total)
    norm_new = nesterov(share.value, norm_momentum, norm_weight, norm_average, rate_norm, token_total)
    return (output, input_grad, *qkv_new, *out_new, *up_new, *down_new, *norm_new)


def solution(mesh):
    dp, ctx = mesh.shape["dp"], mesh.shape["ctx"]
    inner = Mesh(mesh.devices.reshape(dp // 2, 2, ctx), ("chip", "core", "ctx"))
    rows = P(("chip", "core", "ctx"), None)
    cols = P(None, ("chip", "core", "ctx"))
    return jax.shard_map(
        per_device,
        mesh=inner,
        in_specs=(rows, rows, P(("chip", "core"), None)) + (rows,) * 12 + (cols,) * 3,
        out_specs=(rows,) * 14 + (cols,) * 3,
        check_vma=False,
    )
```

```python
import functools
import math

import jax
import jax.numpy as jnp
from jax import lax
from jax.experimental import pallas as pl
from jax.experimental.pallas import tpu as pltpu
from jax.sharding import Mesh, PartitionSpec as P

HEADS = 16
HEAD_DIM = 64
BF = jnp.bfloat16
F32 = jnp.float32
EPS = 1e-05
VMEM_LIMIT = 56 << 20

rate_qkv = 0.04
rate_out = 0.03
rate_up = 0.03
rate_down = 0.02
rate_norm = 0.3

LOG2E = math.log2(math.e)
SCALE = 1.0 / math.sqrt(HEAD_DIM)
NT = (((1,), (1,)), ((), ()))
TN = (((0,), (0,)), ((), ()))


def dot(x, y, dims=None):
    if dims is None:
        return jnp.dot(x, y, preferred_element_type=F32)
    return lax.dot_general(x, y, dims, preferred_element_type=F32)


def call(body, grid, ins, outs, out_shape, args, scratch=(), scalars=0):
    return pl.pallas_call(
        body,
        grid_spec=pltpu.PrefetchScalarGridSpec(
            num_scalar_prefetch=scalars,
            grid=grid,
            in_specs=ins,
            out_specs=outs,
            scratch_shapes=scratch,
        ),
        out_shape=out_shape,
        compiler_params=pltpu.CompilerParams(
            dimension_semantics=("arbitrary",) * len(grid), vmem_limit_bytes=VMEM_LIMIT
        ),
    )(*args)


def shape(rows, cols, dtype):
    return jax.ShapeDtypeStruct((rows, cols), dtype)


def whole(x):
    zeros = (0,) * x.ndim
    return pl.BlockSpec(x.shape, lambda *_: zeros)


def ln_parts(v):
    centre = v - jnp.mean(v, axis=-1, keepdims=True)
    inv = lax.rsqrt(jnp.mean(centre * centre, axis=-1, keepdims=True) + EPS)
    return centre * inv, inv


def ln_grad(xhat, inv, gain, z):
    e = z * gain
    return (
        e - jnp.mean(e, axis=-1, keepdims=True) - xhat * jnp.mean(e * xhat, axis=-1, keepdims=True)
    ) * inv


def column_sums(z, xhat):
    return jnp.concatenate(
        [jnp.sum(z * xhat, axis=0, keepdims=True), jnp.sum(z, axis=0, keepdims=True)], axis=0
    )


def add_to(ref, value):
    @pl.when(pl.program_id(0) == 0)
    def _():
        ref[...] = value

    @pl.when(pl.program_id(0) > 0)
    def _():
        ref[...] += value


def regroup_lanes(u, size):
    lane = lax.broadcasted_iota(jnp.int32, (u.shape[0], 128), 1) % (4 * size)
    groups = []
    for start in range(0, u.shape[1], 128):
        w = u[:, start : start + 128]
        w = jnp.where(
            (lane >= size) & (lane < 2 * size),
            pltpu.roll(w, 128 - size, 1),
            jnp.where((lane >= 2 * size) & (lane < 3 * size), pltpu.roll(w, size, 1), w),
        )
        groups.append(w)
    return jnp.concatenate(groups, axis=1)


def swapped_halves(u):
    lane = lax.broadcasted_iota(jnp.int32, u.shape, 1) % HEAD_DIM
    return jnp.where(lane < HEAD_DIM // 2, pltpu.roll(u, 96, 1), pltpu.roll(u, 32, 1))


def qkv_rows(a, w, cos, sin, q_ref, k_ref, v_ref):
    width = q_ref.shape[1]
    for part, ref in enumerate((q_ref, k_ref)):
        rows = dot(a, w[:, part * width : (part + 1) * width])
        for group in range(width // 128):
            u = rows[:, group * 128 : (group + 1) * 128]
            ref[:, group * 128 : (group + 1) * 128] = (u * cos + swapped_halves(u) * sin).astype(BF)
    v_ref[...] = dot(a, w[:, 2 * width :]).astype(BF)


def first_qkv_body(
    size,
    inverse,
    own_ref,
    other_ref,
    w_ref,
    cos_ref,
    sin_ref,
    a_ref,
    q_ref,
    k_ref,
    v_ref,
):
    owners = w_ref.shape[0]
    x = jnp.where(pl.program_id(0) < 2, own_ref[...], other_ref[...])
    xhat, _ = ln_parts(x.astype(F32))
    norm = jnp.concatenate(
        [
            w_ref[n + side, 2 * size : 2 * size + 8, core * size : (core + 1) * size]
            for n in range(0, owners, 2)
            for core in range(2)
            for side in range(2)
        ],
        axis=1,
    ).astype(F32)
    a = (xhat * norm[0:1, :] + norm[1:2, :]).astype(BF)
    a_ref[...] = a
    w = w_ref[:, : 2 * size, :].reshape(2 * size * owners, w_ref.shape[2])
    qkv_rows(regroup_lanes(a, size), w, cos_ref[...], sin_ref[...], q_ref, k_ref, v_ref)


def next_qkv_body(a_ref, w_ref, cos_ref, sin_ref, q_ref, k_ref, v_ref):
    qkv_rows(a_ref[...], w_ref[...], cos_ref[...], sin_ref[...], q_ref, k_ref, v_ref)


def first_qkv(size, inverse, own, other, w_qkv, cos, sin, span):
    tokens, model = 2 * own.shape[0], own.shape[1]
    width = w_qkv.shape[2] // 3
    row = lambda cols: pl.BlockSpec((span, cols), lambda i, p: (p[i], 0))
    return call(
        functools.partial(first_qkv_body, size),
        (tokens // span,),
        [
            pl.BlockSpec((span, model), lambda i, p: (jnp.minimum(i, 1), 0)),
            pl.BlockSpec((span, model), lambda i, p: (jnp.maximum(i - 2, 0), 0)),
            whole(w_qkv),
            row(128),
            row(128),
        ],
        [row(model), row(width), row(width), row(width)],
        [shape(tokens, model, BF)] + [shape(tokens, width, BF)] * 3,
        (inverse, own, other, w_qkv, cos, sin),
        scalars=1,
    )


def next_qkv(a, w_qkv, cos, sin, span):
    tokens, model = a.shape
    width = w_qkv.shape[1] // 3
    row = lambda cols: pl.BlockSpec((span, cols), lambda i: (i, 0))
    return call(
        next_qkv_body,
        (tokens // span,),
        [row(model), whole(w_qkv), row(128), row(128)],
        [row(width)] * 3,
        [shape(tokens, width, BF)] * 3,
        (a, w_qkv, cos, sin),
    )


def head_mask(shape_):
    return lax.broadcasted_iota(jnp.int32, shape_, 1) < HEAD_DIM


def forward_body(place, q_ref, k_ref, v_ref, own_ref, sent_ref, lse_ref):
    span = own_ref.shape[0] // 2
    first = head_mask((span, 128))
    causal = lax.broadcasted_iota(jnp.int32, (span, span), 0) <= lax.broadcasted_iota(
        jnp.int32, (span, span), 1
    )
    turned = v_ref[...].T
    for block in range(k_ref.shape[0] // span):
        rows = slice(block * span, (block + 1) * span)
        q = q_ref[rows, :]
        zero = jnp.zeros_like(q)
        heads = []
        for head in range(2):
            mine = jnp.where(first, q, zero) if head == 0 else jnp.where(first, zero, q)
            s = dot(k_ref[: rows.stop, :], mine, NT) * (SCALE * LOG2E)
            diagonal = jnp.where(causal, s[rows.start :], -jnp.inf)
            s = jnp.concatenate([s[: rows.start], diagonal], axis=0) if block else diagonal
            top = jnp.max(s, axis=0, keepdims=True)
            p = jnp.exp2(s - top)
            total = jnp.sum(p, axis=0, keepdims=True)
            lanes = slice(head * HEAD_DIM, (head + 1) * HEAD_DIM)
            heads.append(dot(turned[lanes, : rows.stop], p.astype(BF)) / total)
            lse_ref[head * 8 : head * 8 + 1, rows] = top + jnp.log2(total)
        o = jnp.concatenate(heads, axis=0).T.astype(BF)
        at = place[block]

        @pl.when(at < 2)
        def _():
            own_ref[pl.ds(pl.multiple_of(at * span, span), span), :] = o

        @pl.when(at >= 2)
        def _():
            sent_ref[pl.ds(pl.multiple_of((at - 2) * span, span), span), :] = o


def attend_forward(place, q, k, v):
    tokens, width = q.shape
    pairs = width // 128
    full = pl.BlockSpec((tokens, 128), lambda h, p: (0, h))
    half = pl.BlockSpec((tokens // 2, 128), lambda h, p: (0, h))
    return call(
        forward_body,
        (pairs,),
        [full, full, full],
        [half, half, pl.BlockSpec((16, tokens), lambda h, p: (h, 0))],
        [
            shape(tokens // 2, width, BF),
            shape(tokens // 2, width, BF),
            shape(16 * pairs, tokens, F32),
        ],
        (place, q, k, v),
        scalars=1,
    )


def backward_body(
    place,
    q_ref,
    k_ref,
    v_ref,
    own_ref,
    sent_ref,
    g_ref,
    lse_ref,
    cos_ref,
    sin_ref,
    dq_ref,
    dk_ref,
    dv_ref,
    dk_acc,
    dv_acc,
):
    span = own_ref.shape[0] // 2
    rows = span // 2
    first = head_mask((rows, 128))
    zero = jnp.zeros((rows, 128), BF)
    causal = lax.broadcasted_iota(jnp.int32, (rows, rows), 0) <= lax.broadcasted_iota(
        jnp.int32, (rows, rows), 1
    )
    turned = k_ref[...].T
    dk_acc[...] = jnp.zeros_like(dk_acc)
    dv_acc[...] = jnp.zeros_like(dv_acc)
    for block in range(q_ref.shape[0] // rows):
        here = slice(block * rows, (block + 1) * rows)
        at = place[block * rows // span]
        q = q_ref[here, :]
        g = g_ref[pl.ds(pl.multiple_of(at * span + block * rows % span, rows), rows), :]
        start = pl.multiple_of((at % 2) * span + block * rows % span, rows)
        o = jnp.where(at < 2, own_ref[pl.ds(start, rows), :], sent_ref[pl.ds(start, rows), :])
        prod = (o.astype(F32) * g.astype(F32)).T
        parts = []
        for head in range(2):
            lanes = slice(head * HEAD_DIM, (head + 1) * HEAD_DIM)
            q_mine = jnp.where(first, q, zero) if head == 0 else jnp.where(first, zero, q)
            g_mine = jnp.where(first, g, zero) if head == 0 else jnp.where(first, zero, g)
            inner = jnp.sum(prod[lanes], axis=0, keepdims=True)
            s = dot(k_ref[: here.stop, :], q_mine, NT)
            p = jnp.exp2(s * (SCALE * LOG2E) - lse_ref[head * 8 : head * 8 + 1, here])
            diagonal = jnp.where(causal, p[here.start :], 0.0)
            p = jnp.concatenate([p[: here.start], diagonal], axis=0) if block else diagonal
            dp = dot(v_ref[: here.stop, :], g_mine, NT)
            ds = (p * (dp - inner)).astype(BF)
            dv_acc[: here.stop, :] += dot(p.astype(BF), g_mine)
            dk_acc[: here.stop, :] += dot(ds, q_mine)
            parts.append(dot(turned[lanes, : here.stop], ds))
        dq = jnp.concatenate(parts, axis=0).T * SCALE
        dq_ref[here, :] = (dq * cos_ref[here, :] - swapped_halves(dq) * sin_ref[here, :]).astype(BF)
    dk = dk_acc[...] * SCALE
    dk_ref[...] = (dk * cos_ref[...] - swapped_halves(dk) * sin_ref[...]).astype(BF)
    dv_ref[...] = dv_acc[...].astype(BF)


def attend_backward(place, q, k, v, own, sent, g, lse, cos, sin, pair, g_pair):
    tokens = q.shape[0]
    full = pl.BlockSpec((tokens, 128), lambda i, p: (0, pair))
    side = pl.BlockSpec((tokens // 2, 128), lambda i, p: (0, pair))
    out = pl.BlockSpec((tokens, 128), lambda i, p: (0, 0))
    return call(
        backward_body,
        (1,),
        [
            full,
            full,
            full,
            side,
            side,
            pl.BlockSpec((tokens, 128), lambda i, p: (0, g_pair)),
            pl.BlockSpec((16, tokens), lambda i, p: (pair, 0)),
            out,
            out,
        ],
        [out, out, out],
        [shape(tokens, 128, BF)] * 3,
        (place, q, k, v, own, sent, g, lse, cos, sin),
        scratch=[pltpu.VMEM((tokens, 128), F32), pltpu.VMEM((tokens, 128), F32)],
        scalars=1,
    )


def project_body(
    size, m0_ref, m1_ref, o0_ref, o1_ref, wm_ref, wo_ref, x_ref, norm_ref, a_ref, h_ref, c_ref
):
    half = m0_ref.shape[1]
    a = (
        dot(m0_ref[...], wm_ref[:half, :])
        + dot(m1_ref[...], wm_ref[half:, :])
        + dot(o0_ref[...], wo_ref[:half, :])
        + dot(o1_ref[...], wo_ref[half:, :])
    )
    a_ref[...] = a
    xhat, _ = ln_parts(a)
    h = x_ref[...].astype(F32) + (xhat * norm_ref[2:3, :] + norm_ref[3:4, :])
    h_ref[...] = h
    hhat, _ = ln_parts(h)
    c_ref[...] = regroup_lanes((hhat * norm_ref[4:5, :] + norm_ref[5:6, :]).astype(BF), size)


def project(size, mine, other, w_mine, w_other, x, norm, rows=256):
    tokens, model = x.shape
    row = lambda cols: pl.BlockSpec((rows, cols), lambda i: (i, 0))
    half = row(mine[0].shape[1])
    return call(
        functools.partial(project_body, size),
        (tokens // rows,),
        [half] * 4 + [whole(w_mine), whole(w_other), row(model), whole(norm)],
        [row(model)] * 3,
        [shape(tokens, model, F32), shape(tokens, model, F32), shape(tokens, model, BF)],
        (*mine, *other, w_mine, w_other, x, norm),
    )


def turn_body(m_ref, r_ref, h_ref, y_ref, norm_ref, out_ref, dm_ref, sums_ref):
    xhat, inv = ln_parts(m_ref[...] + r_ref[...].astype(F32))
    gain = norm_ref[6:7, :]
    out_ref[...] = (h_ref[...] + (xhat * gain + norm_ref[7:8, :])).astype(BF)
    z = y_ref[...].astype(F32)
    dm_ref[...] = ln_grad(xhat, inv, gain, z).astype(BF)
    add_to(sums_ref, column_sums(z, xhat))


def turn(m_part, m_other, h, y, norm, rows=256):
    tokens, model = y.shape
    row = pl.BlockSpec((rows, model), lambda i: (i, 0))
    return call(
        turn_body,
        (tokens // rows,),
        [row, row, row, row, whole(norm)],
        [row, row, pl.BlockSpec((2, model), lambda i: (0, 0))],
        [shape(tokens, model, BF), shape(tokens, model, BF), shape(2, model, F32)],
        (m_part, m_other, h, y, norm),
    )


def descend_body(
    size, dc_ref, r_ref, h_ref, a_ref, y_ref, norm_ref, dh_ref, da_ref, sums3_ref, sums2_ref
):
    dc = regroup_lanes(dc_ref[...] + r_ref[...].astype(F32), size)
    hhat, inv = ln_parts(h_ref[...])
    dh = y_ref[...].astype(F32) + ln_grad(hhat, inv, norm_ref[4:5, :], dc)
    dh_ref[...] = dh
    add_to(sums3_ref, column_sums(dc, hhat))
    ahat, inv = ln_parts(a_ref[...])
    da_ref[...] = ln_grad(ahat, inv, norm_ref[2:3, :], dh).astype(BF)
    add_to(sums2_ref, column_sums(dh, ahat))


def descend(size, dc_part, dc_other, h, a, y, norm, rows=256):
    tokens, model = y.shape
    row = pl.BlockSpec((rows, model), lambda i: (i, 0))
    sums = pl.BlockSpec((2, model), lambda i: (0, 0))
    return call(
        functools.partial(descend_body, size),
        (tokens // rows,),
        [row] * 5 + [whole(norm)],
        [row, row, sums, sums],
        [
            shape(tokens, model, F32),
            shape(tokens, model, BF),
            shape(2, model, F32),
            shape(2, model, F32),
        ],
        (dc_part, dc_other, h, a, y, norm),
    )


def mlp_weights(w, cols):
    owners, rows, model = w.shape
    down = w.reshape(owners, 2, rows // 2, model)
    up = w.reshape(owners, 4, rows // 4, model)
    per = cols // (rows // 2)
    halves = model // cols
    return (
        [up, down],
        [
            pl.BlockSpec(
                (owners, None, rows // 4, cols), lambda i: (0, 2 + i // halves, 0, i % halves)
            ),
            pl.BlockSpec((per, None, rows // 2, model), lambda i: (i, 0, 0, 0)),
        ],
    )


def flat(ref):
    w = ref[...]
    return w.reshape(w.shape[0] * w.shape[1], w.shape[2])


def add_through(acc, out_ref, value):
    step, last = pl.program_id(0), pl.num_programs(0) - 1

    @pl.when(step == 0)
    def _():
        acc[...] = value

    @pl.when((step > 0) & (step < last))
    def _():
        acc[...] += value

    @pl.when(step == last)
    def _():
        out_ref[...] = (acc[...] + value).astype(out_ref.dtype)


def up_down_body(c_ref, wu_ref, wd_ref, g_ref, s_ref, m_ref, acc):
    u = dot(c_ref[...], flat(wu_ref))
    k = math.sqrt(2.0 / math.pi)
    square = u * u
    t = jnp.tanh(u * (k + (k * 0.044715) * square))
    half = 0.5 + 0.5 * t
    g = (u * half).astype(BF)
    g_ref[...] = g
    s_ref[...] = (
        half + (0.5 * u) * (1.0 - t * t) * (k + (3.0 * k * 0.044715) * square)
    ).astype(BF)
    add_through(acc, m_ref, dot(g, flat(wd_ref)))


def up_down(c, w_mlp, dtype, cols=512):
    tokens, model = c.shape
    units = 2 * model
    wide = pl.BlockSpec((tokens, cols), lambda i: (0, i))
    weights, specs = mlp_weights(w_mlp, cols)
    return call(
        up_down_body,
        (units // cols,),
        [whole(c)] + specs,
        [wide, wide, pl.BlockSpec((tokens, model), lambda i: (0, 0))],
        [shape(tokens, units, BF), shape(tokens, units, BF), shape(tokens, model, dtype)],
        (c, *weights),
        scratch=[pltpu.VMEM((tokens, model), F32)],
    )


def down_up_body(dm_ref, s_ref, wu_ref, wd_ref, du_ref, dc_ref, acc):
    du = (dot(dm_ref[...], flat(wd_ref), NT) * s_ref[...].astype(F32)).astype(BF)
    du_ref[...] = du
    add_through(acc, dc_ref, dot(du, flat(wu_ref), NT))


def down_up(dm, slope, w_mlp, dtype, cols=512):
    tokens, model = dm.shape
    units = 2 * model
    wide = pl.BlockSpec((tokens, cols), lambda i: (0, i))
    weights, specs = mlp_weights(w_mlp, cols)
    return call(
        down_up_body,
        (units // cols,),
        [whole(dm), wide] + specs,
        [wide, pl.BlockSpec((tokens, model), lambda i: (0, 0))],
        [shape(tokens, units, BF), shape(tokens, model, dtype)],
        (dm, slope, *weights),
        scratch=[pltpu.VMEM((tokens, model), F32)],
    )


def other_body(inverse, d0_ref, d1_ref, w0_ref, w1_ref, out_ref):
    out_ref[...] = (dot(d0_ref[...], w0_ref[...], NT) + dot(d1_ref[...], w1_ref[...], NT)).astype(BF)


def own_body(
    inverse, d0_ref, d1_ref, w0_ref, w1_ref, r_ref, x_ref, dh_ref, norm_ref, out_ref, sums_ref
):
    z = dot(d0_ref[...], w0_ref[...], NT) + dot(d1_ref[...], w1_ref[...], NT)
    z = z + r_ref[...].astype(F32)
    xhat, inv = ln_parts(x_ref[...].astype(F32))
    out_ref[...] = (dh_ref[...] + ln_grad(xhat, inv, norm_ref[0:1, :], z)).astype(BF)
    add_to(sums_ref, column_sums(z, xhat))


def input_other(inverse, d, w, span):
    width, model = d[0].shape[1], w[0].shape[0]
    part = pl.BlockSpec((span, width), lambda i, p: (p[i + 2], 0))
    return call(
        other_body,
        (2,),
        [part, part, whole(w[0]), whole(w[1])],
        pl.BlockSpec((span, model), lambda i, p: (i, 0)),
        shape(2 * span, model, BF),
        (inverse, *d, *w),
        scalars=1,
    )


def input_own(inverse, d, w, recv, x, dh, norm, span):
    width, model = d[0].shape[1], w[0].shape[0]
    part = pl.BlockSpec((span, width), lambda i, p: (p[i], 0))
    row = pl.BlockSpec((span, model), lambda i, p: (i, 0))
    return call(
        own_body,
        (2,),
        [part, part, whole(w[0]), whole(w[1]), row, row, row, whole(norm)],
        [row, pl.BlockSpec((2, model), lambda i, p: (0, 0))],
        [shape(2 * span, model, BF), shape(2, model, F32)],
        (inverse, *d, *w, recv, x, dh, norm),
        scalars=1,
    )


def nesterov(gradient, momentum, weight, average, step_rate, token_total):
    scaled = gradient / token_total
    new_momentum = 0.5 * momentum + scaled
    new_weight = weight - step_rate * math.sqrt(token_total) * (scaled + 0.5 * new_momentum)
    new_average = 0.5 * average + 0.5 * new_weight
    return (new_momentum, new_weight, new_average)


def tie(*values):
    return lax.optimization_barrier(values)


def per_device(
    tokens,
    cotangent,
    pair_order,
    qkv_weight,
    qkv_momentum,
    qkv_average,
    out_weight,
    out_momentum,
    out_average,
    up_weight,
    up_momentum,
    up_average,
    down_weight,
    down_momentum,
    down_average,
    norm_weight,
    norm_momentum,
    norm_average,
):
    chips = lax.axis_size("chip")
    ctx_count = lax.axis_size("ctx")
    assert ctx_count == 2 and pair_order.shape[0] == 1 and chips & (chips - 1) == 0
    levels = chips.bit_length() - 1
    chip, core, side = lax.axis_index("chip"), lax.axis_index("core"), lax.axis_index("ctx")
    count, model = tokens.shape
    span = count // 2
    token_total = count * chips * 4
    half = model // 2
    part_heads = HEADS // 4
    rows = qkv_weight.shape[0]
    units = down_weight.shape[0]
    flip = [(0, 1), (1, 0)]

    everyone = ("chip", "core", "ctx")
    full_order = list(range(levels - 1, -1, -1)) + ["core", "ctx"]
    mask_of = {"ctx": 1, "core": 2, **{n: 4 << n for n in range(levels)}}

    def exchange(x, mask):
        return lax.ppermute(x, everyone, [(i, i ^ mask) for i in range(4 * chips)])

    def to_core(x):
        return exchange(x, mask_of["core"])

    def swap_begin(x):
        return lax.ppermute(x, ("core", "ctx"), [(1, 2), (2, 1)])

    def swap_end(x, moved):
        return jnp.where(core == side, x, moved)

    def bit_of(level):
        if level == "ctx":
            return side
        if level == "core":
            return core
        return (chip >> level) & 1

    def pick(x, index, dim):
        return lax.dynamic_index_in_dim(x, index, dim, keepdims=False)

    def by_bit(bit, mine, other, axis=0):
        return jnp.stack(
            [jnp.where(bit == 0, mine, other), jnp.where(bit == 0, other, mine)], axis=axis
        )

    def masks(step):
        result = [0]
        for level in step:
            result = [m for old in result for m in (old, old | mask_of[level])]
        return result

    class Gather:
        def __init__(self, value, steps, names=()):
            self.value, self.names, self.steps = value, list(names), list(steps)

        def send(self):
            self.moved = [exchange(self.value, m) for m in masks(self.steps[0])[1:]]

        def join(self):
            parts = [self.value] + self.moved
            for level in reversed(self.steps.pop(0)):
                dim = sum(full_order.index(n) < full_order.index(level) for n in self.names)
                self.names.insert(dim, level)
                parts = [
                    by_bit(bit_of(level), parts[n], parts[n + 1], dim)
                    for n in range(0, len(parts), 2)
                ]
            (self.value,) = parts

    def tied(gathers, attribute, *rest):
        values, rest = tie([getattr(g, attribute) for g in gathers], rest)
        for g, v in zip(gathers, values):
            setattr(g, attribute, v)
        return rest

    high = list(range(1, levels))
    chain = high[::-1]
    far_steps = [tuple(chain[n : n + 2]) for n in range(0, len(chain), 2)]
    reduce_orders = (
        [(n,) for n in [0, "ctx"] + high],
        [(n,) for n in ["ctx", 0] + high],
    )
    chain = [0, "ctx"] + high
    short_order = [tuple(chain[n : n + 2]) for n in range(0, len(chain), 2)]

    w = qkv_weight.astype(BF).reshape(rows, 3, 2, part_heads, 2, HEAD_DIM)
    norm_low = norm_weight.astype(BF)
    qkv_moved, norm_moved = to_core(pick(w, 1 - core, 4)), to_core(norm_low)
    w_wide = up_weight.astype(BF).reshape(rows, chips, 2, 2 * units)
    up_moved = to_core(pick(w_wide, 1 - core, 2))
    local = by_bit(core, pick(w, core, 4), qkv_moved).transpose(3, 0, 1, 2, 4, 5)
    local = local.reshape(2, 2 * rows, -1)
    norm_local = jnp.pad(
        by_bit(core, norm_low, norm_moved, 1).reshape(8, -1), ((0, 0), (0, local.shape[2] - 2 * rows))
    )
    w_local = out_weight.astype(BF).reshape(rows, 2, half).transpose(1, 0, 2)
    first = Gather(
        jnp.concatenate([local[0], norm_local], axis=0), far_steps + [("ctx",), (0,)]
    )
    second = Gather(
        jnp.concatenate([local[1].reshape(2, rows, -1), w_local], axis=2),
        far_steps + [("ctx",), (0,)],
        ["core"],
    )

    def join_all(gathers, *rest):
        rest = tied(gathers, "moved", *rest)
        for gather in gathers:
            gather.join()
        return tied(gathers, "value", *rest)

    def send_all(gathers):
        for gather in gathers:
            gather.send()

    x_moved = swap_begin(tokens)
    first.send()
    local = by_bit(core, pick(w_wide, core, 2).reshape(rows, 2, -1), up_moved.reshape(rows, 2, -1))
    local = local.transpose(2, 0, 1, 3)
    wide = local.shape[-1]
    per_owner = jnp.concatenate(
        [down_weight.astype(BF).reshape(-1, wide), local.reshape(-1, wide)], axis=0
    )
    positions, order_row, per_owner, x_moved = join_all(
        [first], jnp.arange(2 * count, dtype=jnp.int32), pair_order, per_owner, x_moved
    )
    x = swap_end(tokens, x_moved)
    tied([first, second], "value")
    for _ in far_steps[1:]:
        send_all([first, second])
        join_all([first, second])
    send_all([first] + [second] * (len(far_steps) == 1))
    order_row = jnp.where(core == side, order_row, to_core(order_row))[0]
    mine_first = pick(order_row, core, 0) == 0
    inverse = jnp.where(
        mine_first, jnp.array([0, 3, 1, 2], jnp.int32), jnp.array([1, 2, 0, 3], jnp.int32)
    )
    place = jnp.where(
        mine_first, jnp.array([0, 2, 3, 1], jnp.int32), jnp.array([2, 0, 1, 3], jnp.int32)
    )
    steps = jnp.arange(HEAD_DIM // 2, dtype=F32)
    frequency = jnp.exp(steps * (-math.log(10000.0) / (HEAD_DIM // 2)))
    angles = positions.astype(F32)[:, None] * frequency[None, :]
    cos, sin = jnp.cos(angles), jnp.sin(angles)
    cos_table = jnp.concatenate([cos] * 4, axis=1)
    sin_table = jnp.concatenate([-sin, sin] * 2, axis=1)
    x_other = to_core(x)
    w_mlp = lax.all_gather(per_owner, ("chip", "ctx"), axis=0)
    inverse, place, x_other = join_all(
        [first] + [second] * (len(far_steps) == 1), inverse, place, x_other
    )
    send_all([first, second])
    x_other, cos_table, sin_table, y_out = join_all(
        [first, second], x_other, cos_table, sin_table, cotangent
    )
    second.send()

    a, q0, k0, v0 = first_qkv(
        rows,
        inverse,
        x,
        x_other,
        first.value.reshape(2 * chips, 2 * rows + 8, -1),
        cos_table,
        sin_table,
        span,
    )
    gathered = first.value.reshape(2 * chips, 2 * rows + 8, -1)
    w_first = gathered[:, : 2 * rows].reshape(chips, 2, 2, rows, -1)
    w_first = w_first.transpose(0, 2, 1, 3, 4).reshape(model, -1)
    norm = gathered[:, 2 * rows :, : 2 * rows].reshape(chips, 2, 8, 2, rows)
    norm = norm.transpose(2, 0, 3, 1, 4).reshape(8, model).astype(F32)
    q0, y_out = tie(q0, y_out)
    y_moved = swap_begin(y_out)
    own0, sent0, lse0 = attend_forward(place, q0, k0, v0)
    own0, sent0, a = join_all([second], own0, sent0, a)
    while second.steps:
        second.send()
        own0, sent0, a = join_all([second], own0, sent0, a)
    w_rest = second.value.reshape(chips, 2, 2, rows, -1)
    w_second = w_rest[..., :-half].reshape(model, -1)
    w_out = w_rest[..., -half:].transpose(0, 2, 3, 1, 4).reshape(half, model)
    w_qkv = (w_first, w_second)
    w_out_other = to_core(w_out)
    recv0 = to_core(sent0)
    q1, k1, v1 = next_qkv(a, w_second, cos_table, sin_table, span)
    own1, sent1, lse1 = attend_forward(place, q1, k1, v1)
    own1, sent1, y_moved = tie(own1, sent1, y_moved)
    y = swap_end(cotangent, y_moved)
    recv1 = to_core(sent1)
    projected, hidden, c = project(
        rows, (own0, own1), (recv0, recv1), w_out, w_out_other, x, norm
    )
    c_other = to_core(c)
    g_other, slope_other, m_sent = up_down(c_other, w_mlp, BF)
    m_recv = to_core(m_sent)
    g_mine, slope_mine, m_part = up_down(c, w_mlp, F32)
    output, dm, sums4 = turn(m_part, m_recv, hidden, y, norm)
    output_moved = swap_begin(output)

    class Reduction:
        def __init__(self, value, names, order, wire):
            self.value, self.names, self.order, self.wire = value, names, list(order), wire
            self.flying = False

        def split(self):
            parts = [self.value]
            names = list(self.names)
            for level in self.order[0]:
                dim, bit = names.index(level), bit_of(level)
                names.pop(dim)
                parts = [pick(p, b, dim) for p in parts for b in (bit, 1 - bit)]
            self.names = names
            self.kept, self.moved = parts[0], parts[1:]

        def send(self):
            step = self.order.pop(0)
            self.moved = [exchange(p, m) for p, m in zip(self.moved, masks(step)[1:])]
            self.flying = True

        def add(self):
            v = sum([p.astype(F32) for p in self.moved], self.kept.astype(F32))
            self.value = v.astype(self.wire) if self.order else v
            self.flying = False

    def collect(flying, main):
        flying = [r for r in flying if r.flying]
        moved, main = tie([r.moved for r in flying], main)
        for r, m in zip(flying, moved):
            r.moved = m
            r.add()
        return main

    def launch(started, main):
        started = [r for r in started if r.order and not r.flying]
        for r in started:
            r.split()
        moved, main = tie([r.moved for r in started], main)
        for r, m in zip(started, moved):
            r.moved = m
            r.send()
        return main

    def slot(flying, started, main):
        return launch(flying + started, collect(flying, main))

    def by_rows(g, order, owned):
        names = [n for n in full_order if n != "core" or owned is False]
        return Reduction(g.reshape((2,) * len(names) + (-1, g.shape[1])), names, order, BF)

    def halves(g, owned):
        cut = g.shape[1] // 2
        return [
            by_rows(g[:, n * cut : (n + 1) * cut], reduce_orders[n], owned) for n in range(2)
        ]

    def joined(pair):
        return jnp.concatenate([r.value for r in pair], axis=-1)

    dm_other = to_core(dm)
    du_mine, dc_part = down_up(dm, slope_mine, w_mlp, F32)
    du_other, dc_sent = down_up(dm_other, slope_other, w_mlp, BF)
    du_other, dc_sent, dc_part, output_moved = tie(du_other, dc_sent, dc_part, output_moved)
    output = swap_end(output, output_moved)
    dc_recv = to_core(dc_sent)
    g_two = jnp.concatenate([g_mine, g_other], axis=0)
    dm_two = jnp.concatenate([dm, dm_other], axis=0)
    down_grad = dot(g_two, dm_two, TN).astype(BF)
    down = halves(down_grad, True)
    du_mine, du_other = launch(down, (du_mine, du_other))
    c_two = jnp.concatenate([c, c_other], axis=0)
    du_two = jnp.concatenate([du_mine, du_other], axis=0)
    up_grad, dc_part = tie(dot(c_two, du_two, TN).astype(BF), dc_part)
    up = halves(up_grad, None)
    dh, da, sums3, sums2 = descend(rows, dc_part, dc_recv, hidden, projected, y, norm)
    da = slot(down, up, da)
    da_other = to_core(da)
    da_two = jnp.concatenate([da, da_other], axis=0)
    do = dot(da_two, w_out, NT).astype(BF)
    o_two = jnp.concatenate(
        [jnp.concatenate([own0, own1], axis=1), jnp.concatenate([sent0, sent1], axis=1)], axis=0
    )
    out_grad = jnp.stack(
        [
            dot(o_two, da_two[:, n : n + half], TN).astype(BF).reshape(2**levels, 2, rows, half)
            for n in (0, half)
        ],
        axis=1,
    )
    out_grad, do = tie(out_grad, do)

    def attention_gradient(pair, do):
        q, k, v, own, sent, lse = (
            (q0, k0, v0, own0, sent0, lse0) if pair < 2 else (q1, k1, v1, own1, sent1, lse1)
        )
        return attend_backward(
            place, q, k, v, own, sent, do, lse, cos_table, sin_table, pair % 2, pair
        )

    def weave(first, second):
        return jnp.concatenate([t for pair in zip(first, second) for t in pair], axis=1)

    d0 = attention_gradient(0, do)
    do, d0 = slot(down, [], (do, d0))
    d1 = attention_gradient(1, do)
    do, d1 = slot(down + up, [], (do, d1))
    d_first = weave(d0, d1)
    first_grad = dot(a, d_first, TN).astype(BF).reshape(*out_grad.shape[:-1], -1)
    both = jnp.concatenate([first_grad, out_grad], axis=-1)
    mid = [by_rows(both.reshape(model, -1), short_order, False)]
    d2 = attention_gradient(2, do)
    do, d2 = slot(down + up, mid, (do, d2))
    d3 = slot(down + up + mid, [], attention_gradient(3, do))
    d_second = weave(d2, d3)
    qkv_second = [by_rows(dot(a, d_second, TN).astype(BF), short_order, False)]
    d_second = launch(qkv_second, d_second)
    dx_sent = input_other(inverse, (d_first, d_second), w_qkv, span)
    dx_recv = to_core(dx_sent)
    input_grad, sums1 = input_own(
        inverse, (d_first, d_second), w_qkv, dx_recv, x, dh, norm, span
    )
    input_moved = swap_begin(input_grad)
    norm_grad = jnp.concatenate([sums1, sums2, sums3, sums4], axis=0)
    tiles = norm_grad.reshape(8, -1, rows).transpose(1, 0, 2)
    tiles = lax.all_to_all(tiles, everyone, 0, 0, tiled=True)
    everything = down + up + mid + qkv_second
    tiles = slot(everything, [], tiles)
    while any(r.flying for r in everything):
        tiles = slot(everything, [], tiles)

    def from_cores(part):
        return by_bit(core, pick(part, core, 0), to_core(pick(part, 1 - core, 0)))

    down_sum = joined(down).reshape(units, model)
    out_sum = mid[0].value[..., -half:].reshape(2, rows, half).swapaxes(0, 1).reshape(rows, model)
    up_part = joined(up).reshape(2, rows, chips, 2 * units)
    up_sum = from_cores(up_part).transpose(1, 2, 0, 3).reshape(rows, -1)
    qkv_part = jnp.stack(
        [
            part.reshape(2, rows, 3, part_heads, HEAD_DIM)
            for part in (mid[0].value[..., :-half], qkv_second[0].value)
        ],
        axis=3,
    )
    qkv_sum = from_cores(qkv_part).transpose(1, 2, 3, 4, 0, 5).reshape(rows, -1)
    qkv_new = nesterov(qkv_sum, qkv_momentum, qkv_weight, qkv_average, rate_qkv, token_total)
    out_new = nesterov(out_sum, out_momentum, out_weight, out_average, rate_out, token_total)
    up_new = nesterov(up_sum, up_momentum, up_weight, up_average, rate_up, token_total)
    down_new = nesterov(down_sum, down_momentum, down_weight, down_average, rate_down, token_total)
    qkv_new, up_new, out_new, down_new, tiles, input_moved = tie(
        qkv_new, up_new, out_new, down_new, tiles, input_moved
    )
    norm_sum = jnp.sum(tiles, axis=0)
    input_grad = swap_end(input_grad, input_moved)
    norm_new = nesterov(norm_sum, norm_momentum, norm_weight, norm_average, rate_norm, token_total)
    return (output, input_grad, *qkv_new, *out_new, *up_new, *down_new, *norm_new)


def solution(mesh):
    dp, ctx = mesh.shape["dp"], mesh.shape["ctx"]
    inner = Mesh(mesh.devices.reshape(dp // 2, 2, ctx), ("chip", "core", "ctx"))
    rows = P(("chip", "core", "ctx"), None)
    cols = P(None, ("chip", "core", "ctx"))
    return jax.shard_map(
        per_device,
        mesh=inner,
        in_specs=(rows, rows, P(("chip", "core"), None)) + (rows,) * 12 + (cols,) * 3,
        out_specs=(rows,) * 14 + (cols,) * 3,
        check_vma=False,
    )
```

```python
import functools
import math

import jax
import jax.numpy as jnp
from jax import lax
from jax.experimental import pallas as pl
from jax.experimental.pallas import tpu as pltpu
from jax.sharding import Mesh, PartitionSpec as P

HEADS = 16
HEAD_DIM = 64
BF = jnp.bfloat16
F32 = jnp.float32
EPS = 1e-05
VMEM_LIMIT = 56 << 20

rate_qkv = 0.04
rate_out = 0.03
rate_up = 0.03
rate_down = 0.02
rate_norm = 0.3

LOG2E = math.log2(math.e)
SCALE = 1.0 / math.sqrt(HEAD_DIM)
NT = (((1,), (1,)), ((), ()))
TN = (((0,), (0,)), ((), ()))


def dot(x, y, dims=None):
    if dims is None:
        return jnp.dot(x, y, preferred_element_type=F32)
    return lax.dot_general(x, y, dims, preferred_element_type=F32)


def call(body, grid, ins, outs, out_shape, args, scratch=(), scalars=0):
    return pl.pallas_call(
        body,
        grid_spec=pltpu.PrefetchScalarGridSpec(
            num_scalar_prefetch=scalars,
            grid=grid,
            in_specs=ins,
            out_specs=outs,
            scratch_shapes=scratch,
        ),
        out_shape=out_shape,
        compiler_params=pltpu.CompilerParams(
            dimension_semantics=("arbitrary",) * len(grid), vmem_limit_bytes=VMEM_LIMIT
        ),
    )(*args)


def shape(rows, cols, dtype):
    return jax.ShapeDtypeStruct((rows, cols), dtype)


def whole(x):
    zeros = (0,) * x.ndim
    return pl.BlockSpec(x.shape, lambda *_: zeros)


def ln_parts(v):
    centre = v - jnp.mean(v, axis=-1, keepdims=True)
    inv = lax.rsqrt(jnp.mean(centre * centre, axis=-1, keepdims=True) + EPS)
    return centre * inv, inv


def ln_grad(xhat, inv, gain, z):
    e = z * gain
    return (
        e - jnp.mean(e, axis=-1, keepdims=True) - xhat * jnp.mean(e * xhat, axis=-1, keepdims=True)
    ) * inv


def column_sums(z, xhat):
    return jnp.concatenate(
        [jnp.sum(z * xhat, axis=0, keepdims=True), jnp.sum(z, axis=0, keepdims=True)], axis=0
    )


def add_to(ref, value):
    @pl.when(pl.program_id(0) == 0)
    def _():
        ref[...] = value

    @pl.when(pl.program_id(0) > 0)
    def _():
        ref[...] += value


def regroup_lanes(u, size):
    lane = lax.broadcasted_iota(jnp.int32, (u.shape[0], 128), 1) % (4 * size)
    groups = []
    for start in range(0, u.shape[1], 128):
        w = u[:, start : start + 128]
        w = jnp.where(
            (lane >= size) & (lane < 2 * size),
            pltpu.roll(w, 128 - size, 1),
            jnp.where((lane >= 2 * size) & (lane < 3 * size), pltpu.roll(w, size, 1), w),
        )
        groups.append(w)
    return jnp.concatenate(groups, axis=1)


def swapped_halves(u):
    lane = lax.broadcasted_iota(jnp.int32, u.shape, 1) % HEAD_DIM
    return jnp.where(lane < HEAD_DIM // 2, pltpu.roll(u, 96, 1), pltpu.roll(u, 32, 1))


def qkv_rows(a, w, cos, sin, q_ref, k_ref, v_ref):
    width = q_ref.shape[1]
    for part, ref in enumerate((q_ref, k_ref)):
        rows = dot(a, w[:, part * width : (part + 1) * width])
        for group in range(width // 128):
            u = rows[:, group * 128 : (group + 1) * 128]
            ref[:, group * 128 : (group + 1) * 128] = (u * cos + swapped_halves(u) * sin).astype(BF)
    v_ref[...] = dot(a, w[:, 2 * width :]).astype(BF)


def first_qkv_body(
    size,
    inverse,
    own_ref,
    other_ref,
    w_ref,
    cos_ref,
    sin_ref,
    a_ref,
    q_ref,
    k_ref,
    v_ref,
):
    owners = w_ref.shape[0]
    x = jnp.where(pl.program_id(0) < 2, own_ref[...], other_ref[...])
    xhat, _ = ln_parts(x.astype(F32))
    norm = jnp.concatenate(
        [
            w_ref[n + side, 2 * size : 2 * size + 8, core * size : (core + 1) * size]
            for n in range(0, owners, 2)
            for core in range(2)
            for side in range(2)
        ],
        axis=1,
    ).astype(F32)
    a = (xhat * norm[0:1, :] + norm[1:2, :]).astype(BF)
    a_ref[...] = a
    w = w_ref[:, : 2 * size, :].reshape(2 * size * owners, w_ref.shape[2])
    qkv_rows(regroup_lanes(a, size), w, cos_ref[...], sin_ref[...], q_ref, k_ref, v_ref)


def next_qkv_body(a_ref, w_ref, cos_ref, sin_ref, q_ref, k_ref, v_ref):
    qkv_rows(a_ref[...], w_ref[...], cos_ref[...], sin_ref[...], q_ref, k_ref, v_ref)


def first_qkv(size, inverse, own, other, w_qkv, cos, sin, span):
    tokens, model = 2 * own.shape[0], own.shape[1]
    width = w_qkv.shape[2] // 3
    row = lambda cols: pl.BlockSpec((span, cols), lambda i, p: (p[i], 0))
    return call(
        functools.partial(first_qkv_body, size),
        (tokens // span,),
        [
            pl.BlockSpec((span, model), lambda i, p: (jnp.minimum(i, 1), 0)),
            pl.BlockSpec((span, model), lambda i, p: (jnp.maximum(i - 2, 0), 0)),
            whole(w_qkv),
            row(128),
            row(128),
        ],
        [row(model), row(width), row(width), row(width)],
        [shape(tokens, model, BF)] + [shape(tokens, width, BF)] * 3,
        (inverse, own, other, w_qkv, cos, sin),
        scalars=1,
    )


def next_qkv(a, w_qkv, cos, sin, span):
    tokens, model = a.shape
    width = w_qkv.shape[1] // 3
    row = lambda cols: pl.BlockSpec((span, cols), lambda i: (i, 0))
    return call(
        next_qkv_body,
        (tokens // span,),
        [row(model), whole(w_qkv), row(128), row(128)],
        [row(width)] * 3,
        [shape(tokens, width, BF)] * 3,
        (a, w_qkv, cos, sin),
    )


def head_mask(shape_):
    return lax.broadcasted_iota(jnp.int32, shape_, 1) < HEAD_DIM


def forward_body(place, q_ref, k_ref, v_ref, own_ref, sent_ref, lse_ref):
    span = own_ref.shape[0] // 2
    first = head_mask((span, 128))
    causal = lax.broadcasted_iota(jnp.int32, (span, span), 0) <= lax.broadcasted_iota(
        jnp.int32, (span, span), 1
    )
    turned = v_ref[...].T
    for block in range(k_ref.shape[0] // span):
        rows = slice(block * span, (block + 1) * span)
        q = q_ref[rows, :]
        zero = jnp.zeros_like(q)
        heads = []
        for head in range(2):
            mine = jnp.where(first, q, zero) if head == 0 else jnp.where(first, zero, q)
            s = dot(k_ref[: rows.stop, :], mine, NT) * (SCALE * LOG2E)
            diagonal = jnp.where(causal, s[rows.start :], -jnp.inf)
            s = jnp.concatenate([s[: rows.start], diagonal], axis=0) if block else diagonal
            top = jnp.max(s, axis=0, keepdims=True)
            p = jnp.exp2(s - top)
            total = jnp.sum(p, axis=0, keepdims=True)
            lanes = slice(head * HEAD_DIM, (head + 1) * HEAD_DIM)
            heads.append(dot(turned[lanes, : rows.stop], p.astype(BF)) / total)
            lse_ref[head * 8 : head * 8 + 1, rows] = top + jnp.log2(total)
        o = jnp.concatenate(heads, axis=0).T.astype(BF)
        at = place[block]

        @pl.when(at < 2)
        def _():
            own_ref[pl.ds(pl.multiple_of(at * span, span), span), :] = o

        @pl.when(at >= 2)
        def _():
            sent_ref[pl.ds(pl.multiple_of((at - 2) * span, span), span), :] = o


def attend_forward(place, q, k, v):
    tokens, width = q.shape
    pairs = width // 128
    full = pl.BlockSpec((tokens, 128), lambda h, p: (0, h))
    half = pl.BlockSpec((tokens // 2, 128), lambda h, p: (0, h))
    return call(
        forward_body,
        (pairs,),
        [full, full, full],
        [half, half, pl.BlockSpec((16, tokens), lambda h, p: (h, 0))],
        [
            shape(tokens // 2, width, BF),
            shape(tokens // 2, width, BF),
            shape(16 * pairs, tokens, F32),
        ],
        (place, q, k, v),
        scalars=1,
    )


def backward_body(
    place,
    q_ref,
    k_ref,
    v_ref,
    own_ref,
    sent_ref,
    g_ref,
    lse_ref,
    cos_ref,
    sin_ref,
    dq_ref,
    dk_ref,
    dv_ref,
    dk_acc,
    dv_acc,
):
    span = own_ref.shape[0] // 2
    rows = span // 2
    first = head_mask((rows, 128))
    zero = jnp.zeros((rows, 128), BF)
    causal = lax.broadcasted_iota(jnp.int32, (rows, rows), 0) <= lax.broadcasted_iota(
        jnp.int32, (rows, rows), 1
    )
    turned = k_ref[...].T
    dk_acc[...] = jnp.zeros_like(dk_acc)
    dv_acc[...] = jnp.zeros_like(dv_acc)
    for block in range(q_ref.shape[0] // rows):
        here = slice(block * rows, (block + 1) * rows)
        at = place[block * rows // span]
        q = q_ref[here, :]
        g = g_ref[pl.ds(pl.multiple_of(at * span + block * rows % span, rows), rows), :]
        start = pl.multiple_of((at % 2) * span + block * rows % span, rows)
        o = jnp.where(at < 2, own_ref[pl.ds(start, rows), :], sent_ref[pl.ds(start, rows), :])
        prod = (o.astype(F32) * g.astype(F32)).T
        parts = []
        for head in range(2):
            lanes = slice(head * HEAD_DIM, (head + 1) * HEAD_DIM)
            q_mine = jnp.where(first, q, zero) if head == 0 else jnp.where(first, zero, q)
            g_mine = jnp.where(first, g, zero) if head == 0 else jnp.where(first, zero, g)
            inner = jnp.sum(prod[lanes], axis=0, keepdims=True)
            s = dot(k_ref[: here.stop, :], q_mine, NT)
            p = jnp.exp2(s * (SCALE * LOG2E) - lse_ref[head * 8 : head * 8 + 1, here])
            diagonal = jnp.where(causal, p[here.start :], 0.0)
            p = jnp.concatenate([p[: here.start], diagonal], axis=0) if block else diagonal
            dp = dot(v_ref[: here.stop, :], g_mine, NT)
            ds = (p * (dp - inner)).astype(BF)
            dv_acc[: here.stop, :] += dot(p.astype(BF), g_mine)
            dk_acc[: here.stop, :] += dot(ds, q_mine)
            parts.append(dot(turned[lanes, : here.stop], ds))
        dq = jnp.concatenate(parts, axis=0).T * SCALE
        dq_ref[here, :] = (dq * cos_ref[here, :] - swapped_halves(dq) * sin_ref[here, :]).astype(BF)
    dk = dk_acc[...] * SCALE
    dk_ref[...] = (dk * cos_ref[...] - swapped_halves(dk) * sin_ref[...]).astype(BF)
    dv_ref[...] = dv_acc[...].astype(BF)


def attend_backward(place, q, k, v, own, sent, g, lse, cos, sin, pair, g_pair):
    tokens = q.shape[0]
    full = pl.BlockSpec((tokens, 128), lambda i, p: (0, pair))
    side = pl.BlockSpec((tokens // 2, 128), lambda i, p: (0, pair))
    out = pl.BlockSpec((tokens, 128), lambda i, p: (0, 0))
    return call(
        backward_body,
        (1,),
        [
            full,
            full,
            full,
            side,
            side,
            pl.BlockSpec((tokens, 128), lambda i, p: (0, g_pair)),
            pl.BlockSpec((16, tokens), lambda i, p: (pair, 0)),
            out,
            out,
        ],
        [out, out, out],
        [shape(tokens, 128, BF)] * 3,
        (place, q, k, v, own, sent, g, lse, cos, sin),
        scratch=[pltpu.VMEM((tokens, 128), F32), pltpu.VMEM((tokens, 128), F32)],
        scalars=1,
    )


def project_body(
    size, m0_ref, m1_ref, o0_ref, o1_ref, wm_ref, wo_ref, x_ref, norm_ref, a_ref, h_ref, c_ref
):
    half = m0_ref.shape[1]
    a = (
        dot(m0_ref[...], wm_ref[:half, :])
        + dot(m1_ref[...], wm_ref[half:, :])
        + dot(o0_ref[...], wo_ref[:half, :])
        + dot(o1_ref[...], wo_ref[half:, :])
    )
    a_ref[...] = a
    xhat, _ = ln_parts(a)
    h = x_ref[...].astype(F32) + (xhat * norm_ref[2:3, :] + norm_ref[3:4, :])
    h_ref[...] = h
    hhat, _ = ln_parts(h)
    c_ref[...] = regroup_lanes((hhat * norm_ref[4:5, :] + norm_ref[5:6, :]).astype(BF), size)


def project(size, mine, other, w_mine, w_other, x, norm, rows=256):
    tokens, model = x.shape
    row = lambda cols: pl.BlockSpec((rows, cols), lambda i: (i, 0))
    half = row(mine[0].shape[1])
    return call(
        functools.partial(project_body, size),
        (tokens // rows,),
        [half] * 4 + [whole(w_mine), whole(w_other), row(model), whole(norm)],
        [row(model)] * 3,
        [shape(tokens, model, F32), shape(tokens, model, F32), shape(tokens, model, BF)],
        (*mine, *other, w_mine, w_other, x, norm),
    )


def turn_body(m_ref, r_ref, h_ref, y_ref, norm_ref, out_ref, dm_ref, sums_ref):
    xhat, inv = ln_parts(m_ref[...] + r_ref[...].astype(F32))
    gain = norm_ref[6:7, :]
    out_ref[...] = (h_ref[...] + (xhat * gain + norm_ref[7:8, :])).astype(BF)
    z = y_ref[...].astype(F32)
    dm_ref[...] = ln_grad(xhat, inv, gain, z).astype(BF)
    add_to(sums_ref, column_sums(z, xhat))


def turn(m_part, m_other, h, y, norm, rows=512):
    tokens, model = y.shape
    row = pl.BlockSpec((rows, model), lambda i: (i, 0))
    return call(
        turn_body,
        (tokens // rows,),
        [row, row, row, row, whole(norm)],
        [row, row, pl.BlockSpec((2, model), lambda i: (0, 0))],
        [shape(tokens, model, BF), shape(tokens, model, BF), shape(2, model, F32)],
        (m_part, m_other, h, y, norm),
    )


def descend_body(
    size, dc_ref, r_ref, h_ref, a_ref, y_ref, norm_ref, dh_ref, da_ref, sums3_ref, sums2_ref
):
    dc = regroup_lanes(dc_ref[...] + r_ref[...].astype(F32), size)
    hhat, inv = ln_parts(h_ref[...])
    dh = y_ref[...].astype(F32) + ln_grad(hhat, inv, norm_ref[4:5, :], dc)
    dh_ref[...] = dh
    add_to(sums3_ref, column_sums(dc, hhat))
    ahat, inv = ln_parts(a_ref[...])
    da_ref[...] = ln_grad(ahat, inv, norm_ref[2:3, :], dh).astype(BF)
    add_to(sums2_ref, column_sums(dh, ahat))


def descend(size, dc_part, dc_other, h, a, y, norm, rows=256):
    tokens, model = y.shape
    row = pl.BlockSpec((rows, model), lambda i: (i, 0))
    sums = pl.BlockSpec((2, model), lambda i: (0, 0))
    return call(
        functools.partial(descend_body, size),
        (tokens // rows,),
        [row] * 5 + [whole(norm)],
        [row, row, sums, sums],
        [
            shape(tokens, model, F32),
            shape(tokens, model, BF),
            shape(2, model, F32),
            shape(2, model, F32),
        ],
        (dc_part, dc_other, h, a, y, norm),
    )


def mlp_weights(w, cols):
    owners, rows, model = w.shape
    down = w.reshape(owners, 2, rows // 2, model)
    up = w.reshape(owners, 4, rows // 4, model)
    per = cols // (rows // 2)
    halves = model // cols
    return (
        [up, down],
        [
            pl.BlockSpec(
                (owners, None, rows // 4, cols), lambda i: (0, 2 + i // halves, 0, i % halves)
            ),
            pl.BlockSpec((per, None, rows // 2, model), lambda i: (i, 0, 0, 0)),
        ],
    )


def flat(ref):
    w = ref[...]
    return w.reshape(w.shape[0] * w.shape[1], w.shape[2])


def add_through(acc, out_ref, value):
    step, last = pl.program_id(0), pl.num_programs(0) - 1

    @pl.when(step == 0)
    def _():
        acc[...] = value

    @pl.when((step > 0) & (step < last))
    def _():
        acc[...] += value

    @pl.when(step == last)
    def _():
        out_ref[...] = (acc[...] + value).astype(out_ref.dtype)


def up_down_body(c_ref, wu_ref, wd_ref, g_ref, s_ref, m_ref, acc):
    u = dot(c_ref[...], flat(wu_ref))
    k = math.sqrt(2.0 / math.pi)
    square = u * u
    t = jnp.tanh(u * (k + (k * 0.044715) * square))
    half = 0.5 + 0.5 * t
    g = (u * half).astype(BF)
    g_ref[...] = g
    s_ref[...] = (
        half + (0.5 * u) * (1.0 - t * t) * (k + (3.0 * k * 0.044715) * square)
    ).astype(BF)
    add_through(acc, m_ref, dot(g, flat(wd_ref)))


def up_down(c, w_mlp, dtype, cols=512):
    tokens, model = c.shape
    units = 2 * model
    wide = pl.BlockSpec((tokens, cols), lambda i: (0, i))
    weights, specs = mlp_weights(w_mlp, cols)
    return call(
        up_down_body,
        (units // cols,),
        [whole(c)] + specs,
        [wide, wide, pl.BlockSpec((tokens, model), lambda i: (0, 0))],
        [shape(tokens, units, BF), shape(tokens, units, BF), shape(tokens, model, dtype)],
        (c, *weights),
        scratch=[pltpu.VMEM((tokens, model), F32)],
    )


def down_up_body(dm_ref, s_ref, wu_ref, wd_ref, du_ref, dc_ref, acc):
    du = (dot(dm_ref[...], flat(wd_ref), NT) * s_ref[...].astype(F32)).astype(BF)
    du_ref[...] = du
    add_through(acc, dc_ref, dot(du, flat(wu_ref), NT))


def down_up(dm, slope, w_mlp, dtype, cols=512):
    tokens, model = dm.shape
    units = 2 * model
    wide = pl.BlockSpec((tokens, cols), lambda i: (0, i))
    weights, specs = mlp_weights(w_mlp, cols)
    return call(
        down_up_body,
        (units // cols,),
        [whole(dm), wide] + specs,
        [wide, pl.BlockSpec((tokens, model), lambda i: (0, 0))],
        [shape(tokens, units, BF), shape(tokens, model, dtype)],
        (dm, slope, *weights),
        scratch=[pltpu.VMEM((tokens, model), F32)],
    )


def other_body(inverse, d0_ref, d1_ref, w0_ref, w1_ref, out_ref):
    out_ref[...] = (dot(d0_ref[...], w0_ref[...], NT) + dot(d1_ref[...], w1_ref[...], NT)).astype(BF)


def own_body(
    inverse, d0_ref, d1_ref, w0_ref, w1_ref, r_ref, x_ref, dh_ref, norm_ref, out_ref, sums_ref
):
    z = dot(d0_ref[...], w0_ref[...], NT) + dot(d1_ref[...], w1_ref[...], NT)
    z = z + r_ref[...].astype(F32)
    xhat, inv = ln_parts(x_ref[...].astype(F32))
    out_ref[...] = (dh_ref[...] + ln_grad(xhat, inv, norm_ref[0:1, :], z)).astype(BF)
    add_to(sums_ref, column_sums(z, xhat))


def input_other(inverse, d, w, span):
    width, model = d[0].shape[1], w[0].shape[0]
    part = pl.BlockSpec((span, width), lambda i, p: (p[i + 2], 0))
    return call(
        other_body,
        (2,),
        [part, part, whole(w[0]), whole(w[1])],
        pl.BlockSpec((span, model), lambda i, p: (i, 0)),
        shape(2 * span, model, BF),
        (inverse, *d, *w),
        scalars=1,
    )


def input_own(inverse, d, w, recv, x, dh, norm, span):
    width, model = d[0].shape[1], w[0].shape[0]
    part = pl.BlockSpec((span, width), lambda i, p: (p[i], 0))
    row = pl.BlockSpec((span, model), lambda i, p: (i, 0))
    return call(
        own_body,
        (2,),
        [part, part, whole(w[0]), whole(w[1]), row, row, row, whole(norm)],
        [row, pl.BlockSpec((2, model), lambda i, p: (0, 0))],
        [shape(2 * span, model, BF), shape(2, model, F32)],
        (inverse, *d, *w, recv, x, dh, norm),
        scalars=1,
    )


def nesterov(gradient, momentum, weight, average, step_rate, token_total):
    scaled = gradient / token_total
    new_momentum = 0.5 * momentum + scaled
    new_weight = weight - step_rate * math.sqrt(token_total) * (scaled + 0.5 * new_momentum)
    new_average = 0.5 * average + 0.5 * new_weight
    return (new_momentum, new_weight, new_average)


def tie(*values):
    return lax.optimization_barrier(values)


def per_device(
    tokens,
    cotangent,
    pair_order,
    qkv_weight,
    qkv_momentum,
    qkv_average,
    out_weight,
    out_momentum,
    out_average,
    up_weight,
    up_momentum,
    up_average,
    down_weight,
    down_momentum,
    down_average,
    norm_weight,
    norm_momentum,
    norm_average,
):
    chips = lax.axis_size("chip")
    ctx_count = lax.axis_size("ctx")
    assert ctx_count == 2 and pair_order.shape[0] == 1 and chips & (chips - 1) == 0
    levels = chips.bit_length() - 1
    chip, core, side = lax.axis_index("chip"), lax.axis_index("core"), lax.axis_index("ctx")
    count, model = tokens.shape
    span = count // 2
    token_total = count * chips * 4
    half = model // 2
    part_heads = HEADS // 4
    rows = qkv_weight.shape[0]
    units = down_weight.shape[0]
    flip = [(0, 1), (1, 0)]

    everyone = ("chip", "core", "ctx")
    full_order = list(range(levels - 1, -1, -1)) + ["core", "ctx"]
    mask_of = {"ctx": 1, "core": 2, **{n: 4 << n for n in range(levels)}}

    def exchange(x, mask):
        return lax.ppermute(x, everyone, [(i, i ^ mask) for i in range(4 * chips)])

    def to_core(x):
        return exchange(x, mask_of["core"])

    def swap_begin(x):
        return lax.ppermute(x, ("core", "ctx"), [(1, 2), (2, 1)])

    def swap_end(x, moved):
        return jnp.where(core == side, x, moved)

    def bit_of(level):
        if level == "ctx":
            return side
        if level == "core":
            return core
        return (chip >> level) & 1

    def pick(x, index, dim):
        return lax.dynamic_index_in_dim(x, index, dim, keepdims=False)

    def by_bit(bit, mine, other, axis=0):
        return jnp.stack(
            [jnp.where(bit == 0, mine, other), jnp.where(bit == 0, other, mine)], axis=axis
        )

    def masks(step):
        result = [0]
        for level in step:
            result = [m for old in result for m in (old, old | mask_of[level])]
        return result

    class Gather:
        def __init__(self, value, steps, names=()):
            self.value, self.names, self.steps = value, list(names), list(steps)

        def send(self):
            self.moved = [exchange(self.value, m) for m in masks(self.steps[0])[1:]]

        def join(self):
            parts = [self.value] + self.moved
            for level in reversed(self.steps.pop(0)):
                dim = sum(full_order.index(n) < full_order.index(level) for n in self.names)
                self.names.insert(dim, level)
                parts = [
                    by_bit(bit_of(level), parts[n], parts[n + 1], dim)
                    for n in range(0, len(parts), 2)
                ]
            (self.value,) = parts

    def tied(gathers, attribute, *rest):
        values, rest = tie([getattr(g, attribute) for g in gathers], rest)
        for g, v in zip(gathers, values):
            setattr(g, attribute, v)
        return rest

    high = list(range(1, levels))
    chain = high[::-1]
    far_steps = [tuple(chain[n : n + 2]) for n in range(0, len(chain), 2)]
    reduce_orders = (
        [(n,) for n in [0, "ctx"] + high],
        [(n,) for n in ["ctx", 0] + high],
    )
    chain = [0, "ctx"] + high
    short_order = [tuple(chain[n : n + 2]) for n in range(0, len(chain), 2)]

    w = qkv_weight.astype(BF).reshape(rows, 3, 2, part_heads, 2, HEAD_DIM)
    norm_low = norm_weight.astype(BF)
    qkv_moved, norm_moved = to_core(pick(w, 1 - core, 4)), to_core(norm_low)
    w_wide = up_weight.astype(BF).reshape(rows, chips, 2, 2 * units)
    up_moved = to_core(pick(w_wide, 1 - core, 2))
    local = by_bit(core, pick(w, core, 4), qkv_moved).transpose(3, 0, 1, 2, 4, 5)
    local = local.reshape(2, 2 * rows, -1)
    norm_local = jnp.pad(
        by_bit(core, norm_low, norm_moved, 1).reshape(8, -1), ((0, 0), (0, local.shape[2] - 2 * rows))
    )
    w_local = out_weight.astype(BF).reshape(rows, 2, half).transpose(1, 0, 2)
    first = Gather(
        jnp.concatenate([local[0], norm_local], axis=0), far_steps + [("ctx",), (0,)]
    )
    second = Gather(
        jnp.concatenate([local[1].reshape(2, rows, -1), w_local], axis=2),
        far_steps + [("ctx",), (0,)],
        ["core"],
    )

    def join_all(gathers, *rest):
        rest = tied(gathers, "moved", *rest)
        for gather in gathers:
            gather.join()
        return tied(gathers, "value", *rest)

    def send_all(gathers):
        for gather in gathers:
            gather.send()

    x_moved = swap_begin(tokens)
    first.send()
    local = by_bit(core, pick(w_wide, core, 2).reshape(rows, 2, -1), up_moved.reshape(rows, 2, -1))
    local = local.transpose(2, 0, 1, 3)
    wide = local.shape[-1]
    per_owner = jnp.concatenate(
        [down_weight.astype(BF).reshape(-1, wide), local.reshape(-1, wide)], axis=0
    )
    positions, order_row, per_owner, x_moved = join_all(
        [first], jnp.arange(2 * count, dtype=jnp.int32), pair_order, per_owner, x_moved
    )
    x = swap_end(tokens, x_moved)
    tied([first, second], "value")
    for _ in far_steps[1:]:
        send_all([first, second])
        join_all([first, second])
    send_all([first] + [second] * (len(far_steps) == 1))
    order_row = jnp.where(core == side, order_row, to_core(order_row))[0]
    mine_first = pick(order_row, core, 0) == 0
    inverse = jnp.where(
        mine_first, jnp.array([0, 3, 1, 2], jnp.int32), jnp.array([1, 2, 0, 3], jnp.int32)
    )
    place = jnp.where(
        mine_first, jnp.array([0, 2, 3, 1], jnp.int32), jnp.array([2, 0, 1, 3], jnp.int32)
    )
    steps = jnp.arange(HEAD_DIM // 2, dtype=F32)
    frequency = jnp.exp(steps * (-math.log(10000.0) / (HEAD_DIM // 2)))
    angles = positions.astype(F32)[:, None] * frequency[None, :]
    cos, sin = jnp.cos(angles), jnp.sin(angles)
    cos_table = jnp.concatenate([cos] * 4, axis=1)
    sin_table = jnp.concatenate([-sin, sin] * 2, axis=1)
    x_other = to_core(x)
    w_mlp = lax.all_gather(per_owner, ("chip", "ctx"), axis=0)
    inverse, place, x_other = join_all(
        [first] + [second] * (len(far_steps) == 1), inverse, place, x_other
    )
    send_all([first, second])
    x_other, cos_table, sin_table, y_out = join_all(
        [first, second], x_other, cos_table, sin_table, cotangent
    )
    second.send()

    a, q0, k0, v0 = first_qkv(
        rows,
        inverse,
        x,
        x_other,
        first.value.reshape(2 * chips, 2 * rows + 8, -1),
        cos_table,
        sin_table,
        span,
    )
    gathered = first.value.reshape(2 * chips, 2 * rows + 8, -1)
    w_first = gathered[:, : 2 * rows].reshape(chips, 2, 2, rows, -1)
    w_first = w_first.transpose(0, 2, 1, 3, 4).reshape(model, -1)
    norm = gathered[:, 2 * rows :, : 2 * rows].reshape(chips, 2, 8, 2, rows)
    norm = norm.transpose(2, 0, 3, 1, 4).reshape(8, model).astype(F32)
    q0, y_out = tie(q0, y_out)
    y_moved = swap_begin(y_out)
    own0, sent0, lse0 = attend_forward(place, q0, k0, v0)
    own0, sent0, a = join_all([second], own0, sent0, a)
    while second.steps:
        second.send()
        own0, sent0, a = join_all([second], own0, sent0, a)
    w_rest = second.value.reshape(chips, 2, 2, rows, -1)
    w_second = w_rest[..., :-half].reshape(model, -1)
    w_out = w_rest[..., -half:].transpose(0, 2, 3, 1, 4).reshape(half, model)
    w_qkv = (w_first, w_second)
    w_out_other = to_core(w_out)
    recv0 = to_core(sent0)
    q1, k1, v1 = next_qkv(a, w_second, cos_table, sin_table, span)
    own1, sent1, lse1 = attend_forward(place, q1, k1, v1)
    own1, sent1, y_moved = tie(own1, sent1, y_moved)
    y = swap_end(cotangent, y_moved)
    recv1 = to_core(sent1)
    projected, hidden, c = project(
        rows, (own0, own1), (recv0, recv1), w_out, w_out_other, x, norm
    )
    c_other = to_core(c)
    g_other, slope_other, m_sent = up_down(c_other, w_mlp, BF)
    m_recv = to_core(m_sent)
    g_mine, slope_mine, m_part = up_down(c, w_mlp, F32)
    output, dm, sums4 = turn(m_part, m_recv, hidden, y, norm)
    output_moved = swap_begin(output)

    class Reduction:
        def __init__(self, value, names, order, wire):
            self.value, self.names, self.order, self.wire = value, names, list(order), wire
            self.flying = False

        def split(self):
            parts = [self.value]
            names = list(self.names)
            for level in self.order[0]:
                dim, bit = names.index(level), bit_of(level)
                names.pop(dim)
                parts = [pick(p, b, dim) for p in parts for b in (bit, 1 - bit)]
            self.names = names
            self.kept, self.moved = parts[0], parts[1:]

        def send(self):
            step = self.order.pop(0)
            self.moved = [exchange(p, m) for p, m in zip(self.moved, masks(step)[1:])]
            self.flying = True

        def add(self):
            v = sum([p.astype(F32) for p in self.moved], self.kept.astype(F32))
            self.value = v.astype(self.wire) if self.order else v
            self.flying = False

    def collect(flying, main):
        flying = [r for r in flying if r.flying]
        moved, main = tie([r.moved for r in flying], main)
        for r, m in zip(flying, moved):
            r.moved = m
            r.add()
        return main

    def launch(started, main):
        started = [r for r in started if r.order and not r.flying]
        for r in started:
            r.split()
        moved, main = tie([r.moved for r in started], main)
        for r, m in zip(started, moved):
            r.moved = m
            r.send()
        return main

    def slot(flying, started, main):
        return launch(flying + started, collect(flying, main))

    def by_rows(g, order, owned):
        names = [n for n in full_order if n != "core" or owned is False]
        return Reduction(g.reshape((2,) * len(names) + (-1, g.shape[1])), names, order, BF)

    def halves(g, owned):
        cut = g.shape[1] // 2
        return [
            by_rows(g[:, n * cut : (n + 1) * cut], reduce_orders[n], owned) for n in range(2)
        ]

    def joined(pair):
        return jnp.concatenate([r.value for r in pair], axis=-1)

    dm_other = to_core(dm)
    du_mine, dc_part = down_up(dm, slope_mine, w_mlp, F32)
    du_other, dc_sent = down_up(dm_other, slope_other, w_mlp, BF)
    du_other, dc_sent, dc_part, output_moved = tie(du_other, dc_sent, dc_part, output_moved)
    output = swap_end(output, output_moved)
    dc_recv = to_core(dc_sent)
    g_two = jnp.concatenate([g_mine, g_other], axis=0)
    dm_two = jnp.concatenate([dm, dm_other], axis=0)
    down_grad = dot(g_two, dm_two, TN).astype(BF)
    down = halves(down_grad, True)
    du_mine, du_other = launch(down, (du_mine, du_other))
    c_two = jnp.concatenate([c, c_other], axis=0)
    du_two = jnp.concatenate([du_mine, du_other], axis=0)
    up_grad, dc_part = tie(dot(c_two, du_two, TN).astype(BF), dc_part)
    up = halves(up_grad, None)
    dh, da, sums3, sums2 = descend(rows, dc_part, dc_recv, hidden, projected, y, norm)
    da = slot(down, up, da)
    da_other = to_core(da)
    da_two = jnp.concatenate([da, da_other], axis=0)
    do = dot(da_two, w_out, NT).astype(BF)
    o_two = jnp.concatenate(
        [jnp.concatenate([own0, own1], axis=1), jnp.concatenate([sent0, sent1], axis=1)], axis=0
    )
    out_grad = jnp.stack(
        [
            dot(o_two, da_two[:, n : n + half], TN).astype(BF).reshape(2**levels, 2, rows, half)
            for n in (0, half)
        ],
        axis=1,
    )
    out_grad, do = tie(out_grad, do)

    def attention_gradient(pair, do):
        q, k, v, own, sent, lse = (
            (q0, k0, v0, own0, sent0, lse0) if pair < 2 else (q1, k1, v1, own1, sent1, lse1)
        )
        return attend_backward(
            place, q, k, v, own, sent, do, lse, cos_table, sin_table, pair % 2, pair
        )

    def weave(first, second):
        return jnp.concatenate([t for pair in zip(first, second) for t in pair], axis=1)

    d0 = attention_gradient(0, do)
    do, d0 = slot(down, [], (do, d0))
    d1 = attention_gradient(1, do)
    do, d1 = slot(down + up, [], (do, d1))
    d_first = weave(d0, d1)
    first_grad = dot(a, d_first, TN).astype(BF).reshape(*out_grad.shape[:-1], -1)
    both = jnp.concatenate([first_grad, out_grad], axis=-1)
    mid = [by_rows(both.reshape(model, -1), short_order, False)]
    d2 = attention_gradient(2, do)
    do, d2 = slot(down + up, mid, (do, d2))
    d3 = slot(down + up + mid, [], attention_gradient(3, do))
    d_second = weave(d2, d3)
    qkv_second = [by_rows(dot(a, d_second, TN).astype(BF), short_order, False)]
    d_second = launch(qkv_second, d_second)
    dx_sent = input_other(inverse, (d_first, d_second), w_qkv, span)
    dx_recv = to_core(dx_sent)
    input_grad, sums1 = input_own(
        inverse, (d_first, d_second), w_qkv, dx_recv, x, dh, norm, span
    )
    input_moved = swap_begin(input_grad)
    norm_grad = jnp.concatenate([sums1, sums2, sums3, sums4], axis=0)
    tiles = norm_grad.reshape(8, -1, rows).transpose(1, 0, 2)
    tiles = lax.all_to_all(tiles, everyone, 0, 0, tiled=True)
    everything = down + up + mid + qkv_second
    tiles = slot(everything, [], tiles)
    while any(r.flying for r in everything):
        tiles = slot(everything, [], tiles)

    def from_cores(part):
        return by_bit(core, pick(part, core, 0), to_core(pick(part, 1 - core, 0)))

    down_sum = joined(down).reshape(units, model)
    out_sum = mid[0].value[..., -half:].reshape(2, rows, half).swapaxes(0, 1).reshape(rows, model)
    up_part = joined(up).reshape(2, rows, chips, 2 * units)
    up_sum = from_cores(up_part).transpose(1, 2, 0, 3).reshape(rows, -1)
    qkv_part = jnp.stack(
        [
            part.reshape(2, rows, 3, part_heads, HEAD_DIM)
            for part in (mid[0].value[..., :-half], qkv_second[0].value)
        ],
        axis=3,
    )
    qkv_sum = from_cores(qkv_part).transpose(1, 2, 3, 4, 0, 5).reshape(rows, -1)
    qkv_new = nesterov(qkv_sum, qkv_momentum, qkv_weight, qkv_average, rate_qkv, token_total)
    out_new = nesterov(out_sum, out_momentum, out_weight, out_average, rate_out, token_total)
    up_new = nesterov(up_sum, up_momentum, up_weight, up_average, rate_up, token_total)
    down_new = nesterov(down_sum, down_momentum, down_weight, down_average, rate_down, token_total)
    qkv_new, up_new, out_new, down_new, tiles, input_moved = tie(
        qkv_new, up_new, out_new, down_new, tiles, input_moved
    )
    norm_sum = jnp.sum(tiles, axis=0)
    input_grad = swap_end(input_grad, input_moved)
    norm_new = nesterov(norm_sum, norm_momentum, norm_weight, norm_average, rate_norm, token_total)
    return (output, input_grad, *qkv_new, *out_new, *up_new, *down_new, *norm_new)


def solution(mesh):
    dp, ctx = mesh.shape["dp"], mesh.shape["ctx"]
    inner = Mesh(mesh.devices.reshape(dp // 2, 2, ctx), ("chip", "core", "ctx"))
    rows = P(("chip", "core", "ctx"), None)
    cols = P(None, ("chip", "core", "ctx"))
    return jax.shard_map(
        per_device,
        mesh=inner,
        in_specs=(rows, rows, P(("chip", "core"), None)) + (rows,) * 12 + (cols,) * 3,
        out_specs=(rows,) * 14 + (cols,) * 3,
        check_vma=False,
    )
```
